32 devices in a mesh: rep: 8 (over y, x, core), shard: 4 (over z).
Axes of the slice: x: 2, y: 2, z: 4, core: 2. Of those that a mesh axis runs over, the one named last changes fastest.
Arguments:
- block_input: bfloat16 [2, 5120, 1024], P(None, ('rep', 'shard')), may hold values from -6 to 6
- out_cotangent: bfloat16 [2, 5120, 1024], P(None, ('rep', 'shard')), may hold values from -6 to 6
- segment_ids: int32 [2, 5120], P(None, 'rep'), may hold values from 0 to 12, as said below
- positions: int32 [2, 5120], P(None, 'rep'), may hold values from 0 to 319, as said below
- parent_ids: int32 [2, 8, 13], P(None, 'rep'), may hold values from 0 to 12, as said below
- qkv_weight: float32 [1024, 3072], P('shard'), may hold values from -0.1875 to 0.1875
- attn_weight: float32 [1024, 1024], P('shard'), may hold values from -0.75 to 0.75
- up_weight: float32 [1024, 4096], P('shard'), may hold values from -0.1875 to 0.1875
- down_weight: float32 [4096, 1024], P('shard'), may hold values from -0.09375 to 0.09375
- small_params: float32 [13312], P('shard'), as said below
- qkv_moment: float32 [1024, 3072], P('shard'), may hold values from -448 to 448
- attn_moment: float32 [1024, 1024], P('shard'), may hold values from -96 to 96
- up_moment: float32 [1024, 4096], P('shard'), may hold values from -192 to 192
- down_moment: float32 [4096, 1024], P('shard'), may hold values from -384 to 384
- small_moment: float32 [13312], P('shard'), may hold values from -320 to 320
- qkv_average: float32 [1024, 3072], P('shard'), may hold values from -0.1875 to 0.1875
- attn_average: float32 [1024, 1024], P('shard'), may hold values from -0.75 to 0.75
- up_average: float32 [1024, 4096], P('shard'), may hold values from -0.1875 to 0.1875
- down_average: float32 [4096, 1024], P('shard'), may hold values from -0.09375 to 0.09375
- small_average: float32 [13312], P('shard'), may hold values from 0.5 to 1.5
Outputs:
- block_output: bfloat16 [2, 5120, 1024], P(None, ('rep', 'shard'))
- input_grad: float32 [2, 5120, 1024], P(None, ('rep', 'shard'))
- qkv_grad: float32 [1024, 3072], P('shard')
- attn_grad: float32 [1024, 1024], P('shard')
- up_grad: float32 [1024, 4096], P('shard')
- down_grad: float32 [4096, 1024], P('shard')
- small_grad: float32 [13312], P('shard')
- qkv_state: float32 [2, 1024, 3072], P(None, 'shard')
- attn_state: float32 [2, 1024, 1024], P(None, 'shard')
- up_state: float32 [2, 1024, 4096], P(None, 'shard')
- down_state: float32 [2, 4096, 1024], P(None, 'shard')
- small_state: float32 [2, 13312], P(None, 'shard')
- qkv_momentum: float32 [1024, 3072], P('shard')
- attn_momentum: float32 [1024, 1024], P('shard')
- up_momentum: float32 [1024, 4096], P('shard')
- down_momentum: float32 [4096, 1024], P('shard')
- small_momentum: float32 [13312], P('shard')
The draws below stay inside these ranges and needn't reach their ends.
Inputs may be any that keep to these rules, and one draw needn't show every extreme that they name: `segment_ids`: within each tree the segment numbers never fall along the tokens; the root segment has 256 tokens, every other 32. `positions`: A token's place along its path: root tokens count from 0, a child of the root from 256, a grandchild from 288, each rising by one within its segment. `parent_ids`: the root is its own parent; it has four children, each with two children of its own. `small_params`: gains (the first and third blocks of 1024) near one; biases of both signs.
All inputs are finite; a program needn't handle non-finite values.
Results may differ from the reference program's by a relative error of at most 0.018.
Values may be sent and summed in bfloat16 or wider, within the bound.
No kernel may reach another device: no remote copies, remote signals or barrier semaphores. Data moves between devices by JAX's collectives and lax.ppermute only.
A program may use at most 256 MiB of HBM per device.

```python
import math
import jax
import jax.numpy as jnp
from jax import lax

D = 1024
HEADS = 16
HEAD = 64
ROT = 16
FF = 4096
MB = 2
SEGS = 13
UNIT = 32
TREE = 640
ALL_TOK = 10240
SMALL = 13312
N_REP = 8


def tree_layout(key):
    layout_key = jax.random.fold_in(key, 11)
    tree_keys = jax.random.split(layout_key, MB * N_REP)

    def single_tree(one_key):
        seg_order = jax.random.permutation(one_key, SEGS).astype(jnp.int32)
        lengths = jnp.where(seg_order == 0, 8 * UNIT, UNIT).astype(jnp.int32)
        starts = jnp.cumsum(lengths) - lengths
        slot_ids = jnp.arange(SEGS, dtype=jnp.int32)
        type_slot = jnp.zeros((SEGS,), jnp.int32).at[seg_order].set(slot_ids)
        parent_type = jnp.where(seg_order <= 4, 0, 1 + (seg_order - 5) // 2)
        parents = type_slot[parent_type]
        tokens = jnp.arange(TREE, dtype=jnp.int32)
        segment = jnp.sum((tokens[:, None] >= starts[None, :]).astype(jnp.int32), axis=1) - 1
        seg_kind = seg_order[segment]
        offset = tokens - starts[segment]
        depth_base = jnp.where(seg_kind == 0, 0, jnp.where(seg_kind <= 4, 8 * UNIT, 9 * UNIT))
        return (segment, depth_base + offset, parents)
    segment, token_place, parents = jax.vmap(single_tree)(tree_keys)
    return (segment.reshape(MB, N_REP * TREE).astype(jnp.int32), token_place.reshape(MB, N_REP * TREE).astype(jnp.int32), parents.reshape(MB, N_REP, SEGS).astype(jnp.int32))


def draw_segment_ids(key, part):
    return tree_layout(key)[0]


def draw_positions(key, part):
    return tree_layout(key)[1]


def draw_parent_ids(key, part):
    return tree_layout(key)[2]


def draw_small_params(key, part):
    noise = jax.random.normal(key, (SMALL,), jnp.float32)
    index_all = jnp.arange(SMALL, dtype=jnp.int32)
    gain_slot = (index_all < D) | (index_all >= 2 * D) & (index_all < 3 * D)
    return jnp.where(gain_slot, 1.0 + 0.1 * jnp.clip(noise, -4.0, 4.0), 0.3 * jnp.clip(noise, -5.0, 5.0)).astype(jnp.float32)


def level_of(stream_key, extent, cuts, smallest, high):
    gain = 1.0
    for axis_at, blocks in cuts:
        draws = jax.random.uniform(jax.random.fold_in(jax.random.fold_in(stream_key, 6), axis_at), (blocks,), jnp.float32, smallest / len(cuts), high / len(cuts))
        gain = gain * jnp.repeat(jnp.exp(draws), extent[axis_at] // blocks).reshape((-1,) + (1,) * (len(extent) - 1 - axis_at))
    return gain


def normal_values(key, dims, width, most, cuts=(), kind=jnp.bfloat16):
    factor_of = level_of(key, dims, cuts, -0.22, 0.18) if cuts else 1.0
    values = jax.random.normal(key, dims, jnp.float32) * width * factor_of
    return jnp.minimum(jnp.maximum(values, -most), most).astype(kind)


def setup_inputs(seed: int = 0) -> dict:
    seeds = jax.random.split(jax.random.key(seed), 21)
    block_input = normal_values(seeds[0], (MB, N_REP * TREE, D), 1.0, 6.0, ((1, 32),))
    out_cotangent = normal_values(seeds[1], (MB, N_REP * TREE, D), 1.0, 6.0, ((1, 32),))
    segment_ids = draw_segment_ids(jax.random.fold_in(seeds[20], 71), 0)
    positions = draw_positions(jax.random.fold_in(seeds[20], 71), 0)
    parent_ids = draw_parent_ids(jax.random.fold_in(seeds[20], 71), 0)
    qkv_weight = normal_values(seeds[5], (D, 3 * D), D ** -0.5, 0.1875, ((0, 4),), jnp.float32)
    attn_weight = normal_values(seeds[6], (D, D), (D // 16) ** -0.5, 0.75, ((0, 4),), jnp.float32)
    up_weight = normal_values(seeds[7], (D, FF), D ** -0.5, 0.1875, ((0, 4),), jnp.float32)
    down_weight = normal_values(seeds[8], (FF, D), FF ** -0.5, 0.09375, ((0, 4),), jnp.float32)
    small_params = draw_small_params(jax.random.fold_in(seeds[20], 71), 0)
    qkv_moment = normal_values(seeds[10], (D, 3 * D), (0.7 * ALL_TOK ** 0.5), 448.0, ((0, 4),), jnp.float32)
    attn_moment = normal_values(seeds[11], (D, D), (0.15 * ALL_TOK ** 0.5), 96.0, ((0, 4),), jnp.float32)
    up_moment = normal_values(seeds[12], (D, FF), (0.3 * ALL_TOK ** 0.5), 192.0, ((0, 4),), jnp.float32)
    down_moment = normal_values(seeds[13], (FF, D), (0.65 * ALL_TOK ** 0.5), 384.0, ((0, 4),), jnp.float32)
    small_moment = normal_values(seeds[14], (SMALL,), (0.5 * ALL_TOK ** 0.5), 320.0, ((0, 4),), jnp.float32)
    qkv_average = normal_values(seeds[15], (D, 3 * D), D ** -0.5, 0.1875, ((0, 4),), jnp.float32)
    attn_average = normal_values(seeds[16], (D, D), (D // 16) ** -0.5, 0.75, ((0, 4),), jnp.float32)
    up_average = normal_values(seeds[17], (D, FF), D ** -0.5, 0.1875, ((0, 4),), jnp.float32)
    down_average = normal_values(seeds[18], (FF, D), FF ** -0.5, 0.09375, ((0, 4),), jnp.float32)
    small_average = jnp.clip(1.0 + 0.1 * jax.random.normal(seeds[19], (SMALL,), jnp.float32), 0.5, 1.5)
    return dict(block_input=block_input, out_cotangent=out_cotangent, segment_ids=segment_ids, positions=positions, parent_ids=parent_ids, qkv_weight=qkv_weight, attn_weight=attn_weight, up_weight=up_weight, down_weight=down_weight, small_params=small_params, qkv_moment=qkv_moment, attn_moment=attn_moment, up_moment=up_moment, down_moment=down_moment, small_moment=small_moment, qkv_average=qkv_average, attn_average=attn_average, up_average=up_average, down_average=down_average, small_average=small_average)


@jax.custom_vjp
def low(v):
    return lax.optimization_barrier(v.astype(jnp.bfloat16)).astype(jnp.float32)

@jax.custom_vjp
def low_back(v):
    return v

def low_keep(v):
    return (low(v), None)

def low_pass(kept, grad):
    return (grad,)

def back_keep(v):
    return (v, None)

def back_low(kept, grad):
    return (low(grad),)
low.defvjp(low_keep, low_pass)
low_back.defvjp(back_keep, back_low)
HIGHEST = lax.Precision.HIGHEST
EPSILON = 1e-05
NEGATIVE = -1e+30
MOMENTUM = 0.5
AVERAGE_DECAY = 0.5
RATES = (0.045, 0.8, 0.1, 0.024, 0.4)

def layer_norm(values, gain_vec, bias_vec):
    center = values - lax.optimization_barrier(jnp.mean(values, axis=-1, keepdims=True))
    spread = lax.rsqrt(lax.optimization_barrier(jnp.mean(center * center, axis=-1, keepdims=True)) + EPSILON)
    return center * spread * gain_vec + bias_vec

def rotation(pos_ids):
    half_dims = ROT // 2
    frequency = 10000.0 ** (-(jnp.arange(half_dims, dtype=jnp.float32) * 2.0) / ROT)
    angles = pos_ids.astype(jnp.float32)[:, None] * frequency[None, :]
    return (jnp.cos(angles)[:, None, :], jnp.sin(angles)[:, None, :])

def rotate(tensor, cosine_table, sine_table):
    half_dims = cosine_table.shape[-1]
    first_half = tensor[..., :half_dims]
    second_half = tensor[..., half_dims:2 * half_dims]
    return jnp.concatenate([first_half * cosine_table - second_half * sine_table, second_half * cosine_table + first_half * sine_table, tensor[..., 2 * half_dims:]], axis=-1)

def ancestry(seg_ids, par_ids):
    labels = jnp.arange(SEGS, dtype=jnp.int32)
    parent_tok = par_ids[seg_ids]
    grand_tok = par_ids[parent_tok]
    return ((seg_ids[:, None] == labels[None, :]) | (parent_tok[:, None] == labels[None, :]) | (grand_tok[:, None] == labels[None, :])).astype(jnp.float32)

def attention(query_all, key_all, value_all, anc_all, seg_ids, pos_ids):
    block_len = TREE // 4
    score_scale = HEAD ** (-0.5)

    def one_block(block_item):
        query_block, pos_block, anc_block = block_item
        raw_scores = jnp.einsum('qhd,khd->hqk', query_block, key_all, precision=HIGHEST) * score_scale
        raw_scores = low_back(raw_scores)
        visible = (jnp.take(anc_block, seg_ids, axis=1) > 0.5) & (pos_ids[None, :] <= pos_block[:, None])
        masked = jnp.where(visible[None], raw_scores, NEGATIVE)
        row_top = lax.optimization_barrier(jnp.max(masked, axis=-1, keepdims=True))
        exp_scores = jnp.where(visible[None], jnp.exp(masked - row_top), 0.0)
        probability = low(exp_scores / lax.optimization_barrier(jnp.sum(exp_scores, axis=-1, keepdims=True)))
        return jnp.einsum('hqk,khd->qhd', probability, value_all, precision=HIGHEST)
    blocks = (query_all.reshape(4, block_len, HEADS, HEAD), pos_ids.reshape(4, block_len), anc_all.reshape(4, block_len, SEGS))
    return lax.map(jax.checkpoint(one_block), blocks).reshape(TREE, D)

def tree_forward(tree_input, qkv_w, attn_w, up_w, down_w, small_w, seg_ids, pos_ids, par_ids):
    qkv_w = low(qkv_w)
    attn_w = low(attn_w)
    up_w = low(up_w)
    down_w = low(down_w)
    small_w = low(small_w)
    normed_one = low(layer_norm(tree_input, small_w[:D], small_w[D:2 * D]))
    normed_two = low(layer_norm(tree_input, small_w[2 * D:3 * D], small_w[3 * D:4 * D]))
    qkv_lin = low_back(jnp.dot(normed_one, qkv_w, precision=HIGHEST) + small_w[4 * D:7 * D])
    cosine_table, sine_table = rotation(pos_ids)
    query_all = low(rotate(qkv_lin[:, :D].reshape(TREE, HEADS, HEAD), cosine_table, sine_table))
    key_all = low(rotate(qkv_lin[:, D:2 * D].reshape(TREE, HEADS, HEAD), cosine_table, sine_table))
    value_all = low(qkv_lin[:, 2 * D:].reshape(TREE, HEADS, HEAD))
    anc_all = ancestry(seg_ids, par_ids)
    heads_out = attention(query_all, key_all, value_all, anc_all, seg_ids, pos_ids)
    heads_out = low(low_back(heads_out))
    attn_out = jnp.dot(heads_out, attn_w, precision=HIGHEST) + small_w[7 * D:8 * D]
    up_linear = low_back(jnp.dot(normed_two, up_w, precision=HIGHEST) + small_w[8 * D:8 * D + FF])
    activated = low(jax.nn.gelu(up_linear, approximate=False))
    mlp_out = jnp.dot(activated, down_w, precision=HIGHEST) + small_w[8 * D + FF:]
    return tree_input + attn_out + mlp_out

def reference(block_input, out_cotangent, segment_ids, positions, parent_ids, qkv_weight, attn_weight, up_weight, down_weight, small_params, qkv_moment, attn_moment, up_moment, down_moment, small_moment, qkv_average, attn_average, up_average, down_average, small_average):
    tree_count = MB * N_REP
    tree_inputs = block_input.astype(jnp.float32).reshape(tree_count, TREE, D)
    tree_cots = out_cotangent.astype(jnp.float32).reshape(tree_count, TREE, D)
    seg_all = segment_ids.reshape(tree_count, TREE)
    pos_all = positions.reshape(tree_count, TREE)
    par_all = parent_ids.reshape(tree_count, SEGS)
    masters = (qkv_weight, attn_weight, up_weight, down_weight, small_params)

    def per_tree(grad_totals, tree_item):
        tree_input, tree_cot, seg_ids, pos_ids, par_ids = tree_item

        def forward(values, qkv_w, attn_w, up_w, down_w, small_w):
            return tree_forward(values, qkv_w, attn_w, up_w, down_w, small_w, seg_ids, pos_ids, par_ids)
        result, pullback = jax.vjp(forward, tree_input, *masters)
        gradients = pullback(tree_cot)
        new_totals = tuple((summed + added for summed, added in zip(grad_totals, gradients[1:])))
        return (new_totals, (result.astype(jnp.bfloat16), gradients[0]))
    start_totals = tuple((jnp.zeros_like(master) for master in masters))
    grad_totals, (tree_outs, tree_grads) = lax.scan(per_tree, start_totals, (tree_inputs, tree_cots, seg_all, pos_all, par_all))
    moments = (qkv_moment, attn_moment, up_moment, down_moment, small_moment)
    averages = (qkv_average, attn_average, up_average, down_average, small_average)
    states = []
    new_moments = []
    for weight_index in range(5):
        gradient = grad_totals[weight_index]
        new_moment = MOMENTUM * moments[weight_index] + gradient
        rate_now = RATES[weight_index] / math.sqrt(ALL_TOK)
        new_weight = masters[weight_index] - rate_now * (gradient + MOMENTUM * new_moment)
        new_average = AVERAGE_DECAY * averages[weight_index] + (1.0 - AVERAGE_DECAY) * new_weight
        states.append(jnp.stack([new_weight, new_average]))
        new_moments.append(new_moment)
    return (tree_outs.reshape(MB, N_REP * TREE, D), tree_grads.reshape(MB, N_REP * TREE, D), grad_totals[0], grad_totals[1], grad_totals[2], grad_totals[3], grad_totals[4], states[0], states[1], states[2], states[3], states[4], new_moments[0], new_moments[1], new_moments[2], new_moments[3], new_moments[4])
```

```python
from functools import partial
import math

import jax
import jax.numpy as jnp
from jax import lax
from jax.experimental import pallas as pl
from jax.experimental.pallas import tpu as pltpu
from jax.sharding import PartitionSpec as P

HEAD = 64
ROT = 16
PAIR = 2 * HEAD

EPSILON = 1e-05
NEGATIVE = -1e30
MOMENTUM = 0.5
AVERAGE_DECAY = 0.5
RATES = (0.045, 0.8, 0.1, 0.024, 0.4)

F32 = jnp.float32
BF16 = jnp.bfloat16
VMEM_LIMIT = 60 * 1024 * 1024


def dot(a, b):
    return jnp.dot(a, b, preferred_element_type=F32)


def dot_t(a, b):
    return lax.dot_general(a, b, (((1,), (1,)), ((), ())), preferred_element_type=F32)


def normalize(values):
    center = values - jnp.mean(values, axis=-1, keepdims=True)
    spread = lax.rsqrt(jnp.mean(center * center, axis=-1, keepdims=True) + EPSILON)
    return center * spread, spread


def fixed(shape, index=None):
    zeros = (0,) * len(shape) if index is None else index
    return pl.BlockSpec(shape, lambda i: zeros, pipeline_mode=pl.Buffered(1))


def rows_of(ref):
    block = ref[...]
    return block.reshape(-1, block.shape[-1])


def mlp_kernel(first, reps, shards, *refs):
    if first:
        (x_ref, dy_ref, gain_ref, bias_ref, ub_ref, up_ref, down_ref,
         out_ref, dx_ref, dup_ref, ddown_ref, dub_ref, sums_ref,
         hid, hid_t, unit, acc_out, acc_dx) = refs
    else:
        (x_ref, dy_ref, gain_ref, bias_ref, ub_ref, up_ref, down_ref, pup_ref, pdown_ref, pub_ref,
         out_ref, dx_ref, dup_ref, ddown_ref, dub_ref, sums_ref,
         hid, hid_t, unit, acc_out, acc_dx) = refs
    step = pl.program_id(0)

    @pl.when(step == 0)
    def _():
        xhat, _ = normalize(rows_of(x_ref).astype(F32))
        unit[...] = xhat
        h = (xhat * gain_ref[...] + bias_ref[...]).astype(BF16)
        hid[...] = h
        hid_t[...] = h.T
        acc_out[...] = jnp.zeros_like(acc_out)
        acc_dx[...] = jnp.zeros_like(acc_dx)

    dy = rows_of(dy_ref)
    up = up_ref[...]
    down = down_ref[...]
    u = dot(hid[...], up) + ub_ref[...]
    cdf = 0.5 * (1.0 + lax.erf(u * (0.5 ** 0.5)))
    act = (u * cdf).astype(BF16)
    slope = cdf + u * (jnp.exp(-0.5 * u * u) * ((2.0 * math.pi) ** -0.5))
    dact = dot_t(dy, down)
    du32 = dact * slope
    du = du32.astype(BF16)
    acc_out[...] += dot(act, down)
    acc_dx[...] += dot_t(du, up)
    ddown = dot(act.T, dy)
    dup = dot(hid_t[...], du)
    dub = jnp.sum(du.astype(F32), axis=0, keepdims=True)
    if not first:
        ddown = ddown + pdown_ref[...]
        dub = dub + pub_ref[...]
    ddown_ref[...] = ddown.astype(ddown_ref.dtype)
    dub_ref[...] = dub
    if first:
        dup_ref[...] = dup
    else:
        dup = dup + pup_ref[...]
        part = dup.shape[0] // shards
        for z in range(shards):
            dup_ref[:, z] = dup[z * part:(z + 1) * part].reshape(
                reps, part // reps, dup.shape[1]).astype(BF16)

    @pl.when(step == pl.num_programs(0) - 1)
    def _():
        dh = acc_dx[...]
        out_ref[...] = acc_out[...]
        dx_ref[...] = dh * gain_ref[...]
        sums_ref[0:1] = jnp.sum(dh * unit[...], axis=0, keepdims=True)
        sums_ref[1:2] = jnp.sum(dh, axis=0, keepdims=True)
        sums_ref[2:3] = jnp.sum(dy.astype(F32), axis=0, keepdims=True)
        sums_ref[3:8] = jnp.zeros((5, dh.shape[1]), F32)


def mlp_call(xy, gain, bias, up_bias, weights, down, previous, reps, shards, first_col):
    _, _, rows, width = xy.shape
    tokens = shards * rows
    hidden = down.shape[0]
    block = 256 if hidden % 256 == 0 and first_col % 256 == 0 else 128
    steps = hidden // block
    offset = first_col // block
    first = previous is None
    whole = lambda i: (0, 0)
    in_specs = [
        fixed((shards, 1, rows, width)),
        fixed((shards, 1, rows, width), (0, 1, 0, 0)),
        fixed((1, width)),
        fixed((1, width)),
        pl.BlockSpec((1, block), lambda i: (0, i)),
        pl.BlockSpec((width, block), lambda i: (0, offset + i)),
        pl.BlockSpec((block, width), lambda i: (i, 0)),
    ]
    args = [xy, xy, gain, bias, up_bias, weights, down]
    if first:
        dup_shape = jax.ShapeDtypeStruct((width, hidden), F32)
        dup_spec = pl.BlockSpec((width, block), lambda i: (0, i))
    else:
        in_specs += [
            pl.BlockSpec((width, block), lambda i: (0, i)),
            pl.BlockSpec((block, width), lambda i: (i, 0)),
            pl.BlockSpec((1, block), lambda i: (0, i)),
        ]
        args += list(previous)
        part = width // shards // reps
        dup_shape = jax.ShapeDtypeStruct((reps, shards, part, hidden), BF16)
        dup_spec = pl.BlockSpec((reps, shards, part, block), lambda i: (0, 0, 0, i))
    return pl.pallas_call(
        partial(mlp_kernel, first, reps, shards),
        grid=(steps,),
        in_specs=in_specs,
        out_specs=[
            pl.BlockSpec((tokens, width), whole),
            pl.BlockSpec((tokens, width), whole),
            dup_spec,
            pl.BlockSpec((block, width), lambda i: (i, 0)),
            pl.BlockSpec((1, block), lambda i: (0, i)),
            pl.BlockSpec((8, width), whole),
        ],
        out_shape=[
            jax.ShapeDtypeStruct((tokens, width), F32),
            jax.ShapeDtypeStruct((tokens, width), F32),
            dup_shape,
            jax.ShapeDtypeStruct((hidden, width), F32 if first else BF16),
            jax.ShapeDtypeStruct((1, hidden), F32),
            jax.ShapeDtypeStruct((8, width), F32),
        ],
        scratch_shapes=[
            pltpu.VMEM((tokens, width), BF16),
            pltpu.VMEM((width, tokens), BF16),
            pltpu.VMEM((tokens, width), F32),
            pltpu.VMEM((tokens, width), F32),
            pltpu.VMEM((tokens, width), F32),
        ],
        compiler_params=pltpu.CompilerParams(
            dimension_semantics=("arbitrary",), vmem_limit_bytes=VMEM_LIMIT),
        cost_estimate=pl.CostEstimate(
            flops=12 * tokens * width * hidden, bytes_accessed=24 * 2**20,
            transcendentals=2 * tokens * hidden),
    )(*args)


def swap_halves(values):
    half = ROT // 2
    lane = lax.broadcasted_iota(jnp.int32, values.shape, 1) % HEAD
    return jnp.where(lane < half, pltpu.roll(values, PAIR - half, 1), pltpu.roll(values, half, 1))


def attn_kernel(first, reps, shards, *refs):
    if first:
        (x_ref, dy_ref, gain_ref, bias_ref, cos_ref, sin_ref, mask_ref, qb_ref, qkv_ref, wo_ref,
         out_ref, dx_ref,
         send_ref, dqkv_ref, dwo_ref, dqb_ref, sums_ref,
         hid, hid_t, unit, acc_out, acc_dh) = refs
    else:
        (x_ref, dy_ref, gain_ref, bias_ref, cos_ref, sin_ref, mask_ref, qb_ref, qkv_ref, wo_ref,
         out_ref, dx_ref, pqkv_ref, pwo_ref, pqb_ref,
         send_ref, dqkv_ref, dwo_ref, dqb_ref, sums_ref,
         hid, hid_t, unit, acc_out, acc_dh) = refs
    step = pl.program_id(0)

    @pl.when(step == 0)
    def _():
        xhat, _ = normalize(rows_of(x_ref).astype(F32))
        unit[...] = xhat
        h = (xhat * gain_ref[...] + bias_ref[...]).astype(BF16)
        hid[...] = h
        hid_t[...] = h.T
        acc_out[...] = out_ref[...]
        acc_dh[...] = jnp.zeros_like(acc_dh)

    dy = rows_of(dy_ref)
    weights = qkv_ref[...]
    wo = wo_ref[...]
    cosine = cos_ref[...]
    sine = sin_ref[...]
    lin = dot(hid[...], weights) + qb_ref[...]
    q32 = lin[:, :PAIR]
    k32 = lin[:, PAIR:2 * PAIR]
    q = (q32 * cosine + swap_halves(q32) * sine).astype(BF16) * BF16(HEAD ** -0.5)
    k = (k32 * cosine + swap_halves(k32) * sine).astype(BF16)
    v = lin[:, 2 * PAIR:].astype(BF16)
    do = dot_t(dy, wo).astype(BF16)
    k_t = k.T
    v_t = v.T
    lane = lax.broadcasted_iota(jnp.int32, q.shape, 1)
    o_parts = []
    dq_parts = []
    dk = None
    dv = None
    tokens = q.shape[0]
    chunk = tokens if tokens <= 640 else tokens // 2
    for head in range(2):
        own = (lane // HEAD) == head
        q_h = jnp.where(own, q, jnp.zeros_like(q))
        do_h = jnp.where(own, do, jnp.zeros_like(do))
        part = slice(head * HEAD, (head + 1) * HEAD)
        o_row = []
        dq_row = []
        for at in range(0, tokens, chunk):
            q_c = q_h[at:at + chunk]
            do_c = do_h[at:at + chunk]
            scores = dot_t(k, q_c) + mask_ref[:, at:at + chunk]
            top = jnp.max(scores, axis=0, keepdims=True)
            e = jnp.exp(scores - top)
            prob = e * (1.0 / jnp.sum(e, axis=0, keepdims=True))
            prob_bf = prob.astype(BF16)
            o_row.append(dot(v_t[part], prob_bf))
            dprob = dot_t(v, do_c)
            weighted = prob * dprob
            delta = jnp.sum(weighted, axis=0, keepdims=True)
            ds = (weighted - prob * delta).astype(BF16)
            dq_row.append(dot(k_t[part], ds))
            dk_c = dot(ds, q_c)
            dv_c = dot(prob_bf, do_c)
            dk = dk_c if dk is None else dk + dk_c
            dv = dv_c if dv is None else dv + dv_c
        o_parts.append(jnp.concatenate(o_row, axis=1))
        dq_parts.append(jnp.concatenate(dq_row, axis=1))
    o_t = jnp.concatenate(o_parts, axis=0).astype(BF16)
    dq = jnp.concatenate(dq_parts, axis=0).T * (HEAD ** -0.5)
    dq = dq * cosine - swap_halves(dq) * sine
    dk = dk * cosine - swap_halves(dk) * sine
    dqkv = jnp.concatenate([dq.astype(BF16), dk.astype(BF16), dv.astype(BF16)], axis=1)
    acc_out[...] += dot(o_t.T, wo)
    acc_dh[...] += dot_t(dqkv, weights)
    dwo = dot(o_t, dy)
    dw = dot(hid_t[...], dqkv)
    dqb = jnp.sum(dqkv.astype(F32), axis=0, keepdims=True)
    if first:
        dwo_ref[...] = dwo
        dqkv_ref[...] = dw
        dqb_ref[...] = dqb
    else:
        dwo_ref[...] = (dwo + pwo_ref[...]).astype(BF16)
        dqb_ref[...] = dqb + pqb_ref[...]
        dw = dw + pqkv_ref[...]
        part = dw.shape[0] // shards
        for z in range(shards):
            dqkv_ref[:, z] = dw[z * part:(z + 1) * part].reshape(
                reps, part // reps, dw.shape[1]).astype(BF16)

    @pl.when(step == pl.num_programs(0) - 1)
    def _():
        rows = send_ref.shape[2]
        width = send_ref.shape[3]
        dh = acc_dh[...]
        send_ref[:, 0] = acc_out[...].astype(BF16).reshape(shards, rows, width)
        send_ref[:, 1] = (dx_ref[...] + dh * gain_ref[...]).astype(BF16).reshape(
            shards, rows, width)
        sums_ref[0:1] = jnp.sum(dh * unit[...], axis=0, keepdims=True)
        sums_ref[1:2] = jnp.sum(dh, axis=0, keepdims=True)
        sums_ref[2:8] = jnp.zeros((6, width), F32)


def attn_call(xy, gain, bias, cosine, sine, mask, qkv_bias, weights, wo, partials, previous,
              reps, shards):
    _, _, rows, width = xy.shape
    tokens = shards * rows
    pairs = wo.shape[0] // PAIR
    cols = 3 * PAIR
    first = previous is None
    whole = lambda i: (0, 0)
    in_specs = [
        fixed((shards, 1, rows, width)),
        fixed((shards, 1, rows, width), (0, 1, 0, 0)),
        fixed((1, width)),
        fixed((1, width)),
        fixed((tokens, PAIR)),
        fixed((tokens, PAIR)),
        fixed((tokens, tokens)),
        pl.BlockSpec((1, cols), lambda i: (0, i)),
        pl.BlockSpec((width, cols), lambda i: (0, i)),
        pl.BlockSpec((PAIR, width), lambda i: (i, 0)),
        fixed((tokens, width)),
        fixed((tokens, width)),
    ]
    args = [xy, xy, gain, bias, cosine, sine, mask, qkv_bias, weights, wo, *partials]
    if first:
        dqkv_shape = jax.ShapeDtypeStruct((width, pairs * cols), F32)
        dqkv_spec = pl.BlockSpec((width, cols), lambda i: (0, i))
    else:
        in_specs += [
            pl.BlockSpec((width, cols), lambda i: (0, i)),
            pl.BlockSpec((PAIR, width), lambda i: (i, 0)),
            pl.BlockSpec((1, cols), lambda i: (0, i)),
        ]
        args += list(previous)
        part = width // shards // reps
        dqkv_shape = jax.ShapeDtypeStruct((reps, shards, part, pairs * cols), BF16)
        dqkv_spec = pl.BlockSpec((reps, shards, part, cols), lambda i: (0, 0, 0, i))
    return pl.pallas_call(
        partial(attn_kernel, first, reps, shards),
        grid=(pairs,),
        in_specs=in_specs,
        out_specs=[
            pl.BlockSpec((shards, 2, rows, width), lambda i: (0, 0, 0, 0)),
            dqkv_spec,
            pl.BlockSpec((PAIR, width), lambda i: (i, 0)),
            pl.BlockSpec((1, cols), lambda i: (0, i)),
            pl.BlockSpec((8, width), whole),
        ],
        out_shape=[
            jax.ShapeDtypeStruct((shards, 2, rows, width), BF16),
            dqkv_shape,
            jax.ShapeDtypeStruct((pairs * PAIR, width), F32 if first else BF16),
            jax.ShapeDtypeStruct((1, pairs * cols), F32),
            jax.ShapeDtypeStruct((8, width), F32),
        ],
        scratch_shapes=[
            pltpu.VMEM((tokens, width), BF16),
            pltpu.VMEM((width, tokens), BF16),
            pltpu.VMEM((tokens, width), F32),
            pltpu.VMEM((tokens, width), F32),
            pltpu.VMEM((tokens, width), F32),
        ],
        compiler_params=pltpu.CompilerParams(
            dimension_semantics=("arbitrary",), vmem_limit_bytes=VMEM_LIMIT),
        cost_estimate=pl.CostEstimate(
            flops=pairs * (6 * tokens * width * 4 * PAIR + 28 * tokens * tokens * PAIR),
            bytes_accessed=20 * 2**20, transcendentals=2 * pairs * tokens * tokens),
    )(*args)


def rotation_tables(pos_ids):
    half = ROT // 2
    lane = jnp.arange(PAIR, dtype=jnp.int32) % HEAD
    frequency = 10000.0 ** (-(jnp.arange(half, dtype=F32) * 2.0) / ROT)
    per_lane = jnp.where(lane < ROT, frequency[lane % half], 0.0)
    sign = jnp.where(lane < half, -1.0, jnp.where(lane < ROT, 1.0, 0.0))
    angles = pos_ids.astype(F32)[:, None] * per_lane[None, :]
    return jnp.cos(angles), jnp.sin(angles) * sign[None, :]


def visible_bias(seg_ids, pos_ids, par_ids):
    labels = jnp.arange(par_ids.shape[0], dtype=jnp.int32)
    own = seg_ids[:, None] == labels[None, :]
    parent = jnp.sum(jnp.where(own, par_ids[None, :], 0), axis=1)
    parent_hot = parent[:, None] == labels[None, :]
    grand = jnp.sum(jnp.where(parent_hot, par_ids[None, :], 0), axis=1)
    key_seg = seg_ids[:, None]
    reach = (
        (key_seg == seg_ids[None, :])
        | (key_seg == parent[None, :])
        | (key_seg == grand[None, :])
    )
    return jnp.where(reach & (pos_ids[:, None] <= pos_ids[None, :]), 0.0, NEGATIVE).astype(F32)


def local(
    block_input,
    out_cotangent,
    segment_ids,
    positions,
    parent_ids,
    qkv_weight,
    attn_weight,
    up_weight,
    down_weight,
    small_params,
    qkv_moment,
    attn_moment,
    up_moment,
    down_moment,
    small_moment,
    qkv_average,
    attn_average,
    up_average,
    down_average,
    small_average,
):
    shards = lax.axis_size("shard")
    reps = lax.axis_size("rep")
    me = lax.axis_index("rep")
    z = lax.axis_index("shard")
    micro_count, rows, width = block_input.shape
    hidden = up_weight.shape[1]
    part = qkv_weight.shape[0] // reps
    slice_ff = hidden // shards
    slice_d = width // shards
    pairs = slice_d // PAIR
    qkv_cols = 3 * slice_d

    qkv_rows = lax.dynamic_slice_in_dim(qkv_weight, me * part, part, 0).astype(BF16)
    up_rows = lax.dynamic_slice_in_dim(up_weight, me * part, part, 0).astype(BF16)
    qkv_rows = qkv_rows.reshape(part, 3, shards, pairs, PAIR).transpose(2, 0, 3, 1, 4)
    up_rows = up_rows.reshape(part, shards, slice_ff).transpose(1, 0, 2)
    outgoing = jnp.concatenate([qkv_rows.reshape(shards, part, qkv_cols), up_rows], axis=2)
    arrived = lax.all_to_all(outgoing, "shard", 0, 0, tiled=False)
    weights = lax.all_gather(arrived, "rep", axis=1).reshape(width, qkv_cols + slice_ff)
    down_bf = down_weight.astype(BF16)
    attn_bf = attn_weight.astype(BF16)

    small_full = lax.all_gather(small_params.astype(BF16), "shard", axis=0, tiled=True).astype(F32)
    gain_one, bias_one, gain_two, bias_two = (
        small_full[i * width:(i + 1) * width].reshape(1, width) for i in range(4))
    qkv_bias = small_full[4 * width:7 * width].reshape(3, shards, pairs, PAIR)
    qkv_bias = lax.dynamic_index_in_dim(qkv_bias, z, 1, keepdims=False)
    qkv_bias = qkv_bias.transpose(1, 0, 2).reshape(1, qkv_cols)
    attn_bias = small_full[7 * width:8 * width]
    up_bias = lax.dynamic_slice_in_dim(
        small_full[8 * width:8 * width + hidden], z * slice_ff, slice_ff, 0).reshape(1, slice_ff)
    down_bias = small_full[8 * width + hidden:]

    mlp_previous = None
    attn_previous = None
    sums_two = 0.0
    sums_one = 0.0
    summed = []
    for m in range(micro_count):
        pair = jnp.stack([block_input[m], out_cotangent[m]])
        xy = lax.all_gather(pair, "shard", axis=0)
        cosine, sine = rotation_tables(positions[m])
        mask = visible_bias(segment_ids[m], positions[m], parent_ids[m, 0])
        out_part, dx_part, *mlp_previous, sums = mlp_call(
            xy, gain_two, bias_two, up_bias, weights, down_bf, mlp_previous, reps, shards, qkv_cols)
        sums_two = sums_two + sums
        send, *attn_previous, sums = attn_call(
            xy, gain_one, bias_one, cosine, sine, mask, qkv_bias, weights, attn_bf,
            (out_part, dx_part), attn_previous, reps, shards)
        sums_one = sums_one + sums
        summed.append(lax.psum_scatter(send, "shard", scatter_dimension=0, tiled=False))

    grad_up, grad_down, grad_up_bias = mlp_previous
    grad_qkv, grad_attn, grad_qkv_bias = attn_previous

    grad_down = lax.psum_scatter(
        grad_down.reshape(reps, -1, width), "rep", scatter_dimension=0, tiled=False)
    grad_attn = lax.psum_scatter(
        grad_attn.reshape(reps, -1, width), "rep", scatter_dimension=0, tiled=False)
    grad_up = lax.psum_scatter(grad_up, "rep", scatter_dimension=0, tiled=False)
    grad_qkv = lax.psum_scatter(grad_qkv, "rep", scatter_dimension=0, tiled=False)
    grad_up = lax.all_to_all(grad_up, "shard", 0, 0, tiled=False)
    grad_qkv = lax.all_to_all(grad_qkv, "shard", 0, 0, tiled=False)
    full_down = lax.all_gather(grad_down, "rep", axis=0, tiled=True)
    full_attn = lax.all_gather(grad_attn, "rep", axis=0, tiled=True)
    full_up = lax.all_gather(grad_up, "rep", axis=0).transpose(0, 2, 1, 3).reshape(-1, hidden)
    full_qkv = lax.all_gather(grad_qkv, "rep", axis=0)
    full_qkv = full_qkv.reshape(reps, shards, part, pairs, 3, PAIR).transpose(0, 2, 4, 1, 3, 5)
    full_qkv = full_qkv.reshape(-1, 3 * width)

    head_part = jnp.concatenate(
        [sums_one[0], sums_one[1], sums_two[0], sums_two[1]])
    bias_part = lax.dynamic_update_slice(
        jnp.zeros((3, shards, slice_d), F32),
        grad_qkv_bias.reshape(pairs, 3, PAIR).transpose(1, 0, 2).reshape(3, 1, slice_d),
        (0, z, 0)).reshape(-1)
    token_part = jnp.where(z == 0, sums_two[2], 0.0)
    ff_part = lax.dynamic_update_slice(
        jnp.zeros((hidden,), F32), grad_up_bias.reshape(-1), (z * slice_ff,))
    small_grad = lax.psum(
        jnp.concatenate([head_part, bias_part, token_part, ff_part, token_part]), ("rep", "shard"))
    count = small_params.shape[0]
    small_grad = lax.dynamic_slice_in_dim(small_grad, z * count, count, 0)

    block_outputs = []
    input_grads = []
    for m in range(micro_count):
        x32 = block_input[m].astype(F32)
        block_outputs.append(
            (x32 + summed[m][0].astype(F32) + (attn_bias + down_bias)[None, :]).astype(BF16))
        unit, spread = normalize(x32)
        scaled = summed[m][1].astype(F32)
        input_grads.append(
            out_cotangent[m].astype(F32) + spread * (
                scaled - jnp.mean(scaled, axis=-1, keepdims=True)
                - unit * jnp.mean(scaled * unit, axis=-1, keepdims=True)))

    grads = [full_qkv.astype(F32), full_attn.astype(F32), full_up.astype(F32),
             full_down.astype(F32), small_grad]
    all_tok = micro_count * rows * shards * reps
    masters = (qkv_weight, attn_weight, up_weight, down_weight, small_params)
    moments = (qkv_moment, attn_moment, up_moment, down_moment, small_moment)
    averages = (qkv_average, attn_average, up_average, down_average, small_average)
    states = []
    new_moments = []
    for weight_index in range(5):
        gradient = grads[weight_index]
        new_moment = MOMENTUM * moments[weight_index] + gradient
        rate_now = RATES[weight_index] / math.sqrt(all_tok)
        new_weight = masters[weight_index] - rate_now * (gradient + MOMENTUM * new_moment)
        new_average = AVERAGE_DECAY * averages[weight_index] + (1.0 - AVERAGE_DECAY) * new_weight
        states.append(jnp.stack([new_weight, new_average]))
        new_moments.append(new_moment)
    return (
        jnp.stack(block_outputs),
        jnp.stack(input_grads),
        *grads,
        *states,
        *new_moments,
    )


def solution(mesh):
    tokens = P(None, ("rep", "shard"), None)
    tree = P(None, "rep")
    matrix = P("shard", None)
    vector = P("shard")
    weights = (matrix, matrix, matrix, matrix, vector)
    state = P(None, "shard", None)
    return jax.shard_map(
        local,
        mesh=mesh,
        in_specs=(tokens, tokens, tree, tree, P(None, "rep", None), *weights, *weights, *weights),
        out_specs=(tokens, tokens, *weights, state, state, state, state, P(None, "shard"),
                   *weights),
        check_vma=False,
    )
```

```python
from functools import partial
import math

import jax
import jax.numpy as jnp
from jax import lax
from jax.experimental import pallas as pl
from jax.experimental.pallas import tpu as pltpu
from jax.sharding import PartitionSpec as P

HEAD = 64
ROT = 16
PAIR = 2 * HEAD
LANES = 128

EPSILON = 1e-05
NEGATIVE = -1e30
MOMENTUM = 0.5
AVERAGE_DECAY = 0.5
RATES = (0.045, 0.8, 0.1, 0.024, 0.4)

F32 = jnp.float32
BF16 = jnp.bfloat16
VMEM_LIMIT = 60 * 1024 * 1024


def dot(a, b):
    return jnp.dot(a, b, preferred_element_type=F32)


def dot_t(a, b):
    return lax.dot_general(a, b, (((1,), (1,)), ((), ())), preferred_element_type=F32)


def normalize(values):
    center = values - jnp.mean(values, axis=-1, keepdims=True)
    spread = lax.rsqrt(jnp.mean(center * center, axis=-1, keepdims=True) + EPSILON)
    return center * spread, spread


def fixed(shape, index=None):
    zeros = (0,) * len(shape) if index is None else index
    return pl.BlockSpec(shape, lambda *_: zeros, pipeline_mode=pl.Buffered(1))


def rows_of(ref):
    block = ref[...]
    return block.reshape(-1, block.shape[-1])


def mlp_kernel(first, reps, shards, where_ref, *refs):
    if first:
        (x_ref, dy_ref, gain_ref, bias_ref, ub_ref, up_ref, down_ref,
         out_ref, dx_ref, dup_ref, ddown_ref, dub_ref, sums_ref,
         hid, hid_t, unit, acc_out, acc_dx) = refs
    else:
        (x_ref, dy_ref, gain_ref, bias_ref, ub_ref, up_ref, down_ref, pup_ref, pdown_ref, pub_ref,
         out_ref, dx_ref, keep_ref, give_ref, dub_ref, sums_ref,
         hid, hid_t, unit, acc_out, acc_dx, dup_buf, ddown_buf) = refs
    step = pl.program_id(0)

    @pl.when(step == 0)
    def _():
        xhat, _ = normalize(rows_of(x_ref).astype(F32))
        unit[...] = xhat
        h = (xhat * gain_ref[...] + bias_ref[...]).astype(BF16)
        hid[...] = h
        hid_t[...] = h.T
        acc_out[...] = jnp.zeros_like(acc_out)
        acc_dx[...] = jnp.zeros_like(acc_dx)

    dy = rows_of(dy_ref)
    up = up_ref[...]
    down = down_ref[...]
    u = dot(hid[...], up) + ub_ref[...]
    cdf = 0.5 * (1.0 + lax.erf(u * (0.5 ** 0.5)))
    act = (u * cdf).astype(BF16)
    slope = cdf + u * (jnp.exp(-0.5 * u * u) * ((2.0 * math.pi) ** -0.5))
    dact = dot_t(dy, down)
    du32 = dact * slope
    du = du32.astype(BF16)
    acc_out[...] += dot(act, down)
    acc_dx[...] += dot_t(du, up)
    ddown = dot(act.T, dy)
    dup = dot(hid_t[...], du)
    dub = jnp.sum(du.astype(F32), axis=0, keepdims=True)
    if first:
        ddown_ref[...] = ddown
        dub_ref[...] = dub
        dup_ref[...] = dup
    else:
        dub_ref[...] = dub + pub_ref[...]
        dup_buf[...] = dup + pup_ref[...]
        ddown_buf[...] = ddown + pdown_ref[...]
        width, block = dup_buf.shape
        steps = pl.num_programs(0)
        part = width // shards // reps
        tiles = block // LANES
        line = block // reps
        up_rows = shards * steps * tiles * part
        for j in range(reps):
            piece = where_ref[0] ^ j
            out = keep_ref.at[j] if j < reps // 2 else give_ref.at[j - reps // 2]
            for zz in range(shards):
                row = (where_ref[1] ^ zz) * (width // shards) + piece * part
                value = dup_buf[pl.ds(pl.multiple_of(row, part), part), :].astype(BF16)
                for t in range(tiles):
                    at = ((zz * steps + step) * tiles + t) * part
                    out[pl.ds(pl.multiple_of(at, part), part), :] = (
                        value[:, t * LANES:(t + 1) * LANES])
            value = ddown_buf[pl.ds(pl.multiple_of(piece * line, line), line), :].astype(BF16)
            for t in range(width // LANES):
                at = up_rows + (step * (width // LANES) + t) * line
                out[pl.ds(pl.multiple_of(at, line), line), :] = value[:, t * LANES:(t + 1) * LANES]

    @pl.when(step == pl.num_programs(0) - 1)
    def _():
        dh = acc_dx[...]
        out_ref[...] = acc_out[...]
        dx_ref[...] = dh * gain_ref[...]
        sums_ref[0:1] = jnp.sum(dh * unit[...], axis=0, keepdims=True)
        sums_ref[1:2] = jnp.sum(dh, axis=0, keepdims=True)
        sums_ref[2:3] = jnp.sum(dy.astype(F32), axis=0, keepdims=True)
        sums_ref[3:8] = jnp.zeros((5, dh.shape[1]), F32)


def mlp_call(where, xy, gain, bias, up_bias, weights, down, previous, reps, shards, first_col):
    _, _, rows, width = xy.shape
    tokens = shards * rows
    hidden = down.shape[0]
    block = 256 if hidden % 256 == 0 and first_col % 256 == 0 else 128
    steps = hidden // block
    offset = first_col // block
    first = previous is None
    whole = lambda i, *_: (0, 0)
    in_specs = [
        fixed((shards, 1, rows, width)),
        fixed((shards, 1, rows, width), (0, 1, 0, 0)),
        fixed((1, width)),
        fixed((1, width)),
        pl.BlockSpec((1, block), lambda i, *_: (0, i)),
        pl.BlockSpec((width, block), lambda i, *_: (0, offset + i)),
        pl.BlockSpec((block, width), lambda i, *_: (i, 0)),
    ]
    args = [xy, xy, gain, bias, up_bias, weights, down]
    if first:
        grad_shapes = [jax.ShapeDtypeStruct((width, hidden), F32),
                       jax.ShapeDtypeStruct((hidden, width), F32)]
        grad_specs = [pl.BlockSpec((width, block), lambda i, *_: (0, i)),
                      pl.BlockSpec((block, width), lambda i, *_: (i, 0))]
        buffers = []
    else:
        in_specs += [
            pl.BlockSpec((width, block), lambda i, *_: (0, i)),
            pl.BlockSpec((block, width), lambda i, *_: (i, 0)),
            pl.BlockSpec((1, block), lambda i, *_: (0, i)),
        ]
        args += list(previous)
        pieces = (reps // 2, 2 * width * hidden // reps // LANES, LANES)
        grad_shapes = [jax.ShapeDtypeStruct(pieces, BF16)] * 2
        grad_specs = [pl.BlockSpec(pieces, lambda i, *_: (0, 0, 0))] * 2
        buffers = [pltpu.VMEM((width, block), F32), pltpu.VMEM((block, width), F32)]
    return pl.pallas_call(
        partial(mlp_kernel, first, reps, shards),
        grid_spec=pltpu.PrefetchScalarGridSpec(
            num_scalar_prefetch=1, grid=(steps,),
            in_specs=in_specs,
            out_specs=[
            pl.BlockSpec((tokens, width), whole),
            pl.BlockSpec((tokens, width), whole),
            *grad_specs,
            pl.BlockSpec((1, block), lambda i, *_: (0, i)),
            pl.BlockSpec((8, width), whole),
        ],
            scratch_shapes=[
                pltpu.VMEM((tokens, width), BF16),
                pltpu.VMEM((width, tokens), BF16),
                pltpu.VMEM((tokens, width), F32),
                pltpu.VMEM((tokens, width), F32),
                pltpu.VMEM((tokens, width), F32),
                *buffers,
            ]),
        out_shape=[
            jax.ShapeDtypeStruct((tokens, width), F32),
            jax.ShapeDtypeStruct((tokens, width), F32),
            *grad_shapes,
            jax.ShapeDtypeStruct((1, hidden), F32),
            jax.ShapeDtypeStruct((8, width), F32),
        ],
        compiler_params=pltpu.CompilerParams(
            dimension_semantics=("arbitrary",), vmem_limit_bytes=VMEM_LIMIT),
        cost_estimate=pl.CostEstimate(
            flops=12 * tokens * width * hidden, bytes_accessed=24 * 2**20,
            transcendentals=2 * tokens * hidden),
    )(where, *args)


def swap_halves(values):
    half = ROT // 2
    lane = lax.broadcasted_iota(jnp.int32, values.shape, 1) % HEAD
    return jnp.where(lane < half, pltpu.roll(values, PAIR - half, 1), pltpu.roll(values, half, 1))


def attn_kernel(first, reps, shards, where_ref, *refs):
    if first:
        (x_ref, dy_ref, gain_ref, bias_ref, cos_ref, sin_ref, mask_ref, qb_ref, qkv_ref, wo_ref,
         out_ref, dx_ref,
         send_ref, dqkv_ref, dwo_ref, dqb_ref, sums_ref,
         hid, hid_t, unit, acc_out, acc_dh) = refs
    else:
        (x_ref, dy_ref, gain_ref, bias_ref, cos_ref, sin_ref, mask_ref, qb_ref, qkv_ref, wo_ref,
         out_ref, dx_ref, pqkv_ref, pwo_ref, pqb_ref,
         send_ref, keep_ref, give_ref, dqb_ref, sums_ref,
         hid, hid_t, unit, acc_out, acc_dh, dqkv_buf, dwo_buf) = refs
    step = pl.program_id(0)

    @pl.when(step == 0)
    def _():
        xhat, _ = normalize(rows_of(x_ref).astype(F32))
        unit[...] = xhat
        h = (xhat * gain_ref[...] + bias_ref[...]).astype(BF16)
        hid[...] = h
        hid_t[...] = h.T
        acc_out[...] = out_ref[...]
        acc_dh[...] = jnp.zeros_like(acc_dh)

    dy = rows_of(dy_ref)
    weights = qkv_ref[...]
    wo = wo_ref[...]
    cosine = cos_ref[...]
    sine = sin_ref[...]
    lin = dot(hid[...], weights) + qb_ref[...]
    q32 = lin[:, :PAIR]
    k32 = lin[:, PAIR:2 * PAIR]
    q = (q32 * cosine + swap_halves(q32) * sine).astype(BF16) * BF16(HEAD ** -0.5)
    k = (k32 * cosine + swap_halves(k32) * sine).astype(BF16)
    v = lin[:, 2 * PAIR:].astype(BF16)
    do = dot_t(dy, wo).astype(BF16)
    k_t = k.T
    v_t = v.T
    lane = lax.broadcasted_iota(jnp.int32, q.shape, 1)
    o_parts = []
    dq_parts = []
    dk = None
    dv = None
    tokens = q.shape[0]
    chunk = tokens if tokens <= 640 else tokens // 2
    for head in range(2):
        own = (lane // HEAD) == head
        q_h = jnp.where(own, q, jnp.zeros_like(q))
        do_h = jnp.where(own, do, jnp.zeros_like(do))
        part = slice(head * HEAD, (head + 1) * HEAD)
        o_row = []
        dq_row = []
        for at in range(0, tokens, chunk):
            q_c = q_h[at:at + chunk]
            do_c = do_h[at:at + chunk]
            scores = dot_t(k, q_c) + mask_ref[:, at:at + chunk]
            top = jnp.max(scores, axis=0, keepdims=True)
            e = jnp.exp(scores - top)
            prob = e * (1.0 / jnp.sum(e, axis=0, keepdims=True))
            prob_bf = prob.astype(BF16)
            o_row.append(dot(v_t[part], prob_bf))
            dprob = dot_t(v, do_c)
            weighted = prob * dprob
            delta = jnp.sum(weighted, axis=0, keepdims=True)
            ds = (weighted - prob * delta).astype(BF16)
            dq_row.append(dot(k_t[part], ds))
            dk_c = dot(ds, q_c)
            dv_c = dot(prob_bf, do_c)
            dk = dk_c if dk is None else dk + dk_c
            dv = dv_c if dv is None else dv + dv_c
        o_parts.append(jnp.concatenate(o_row, axis=1))
        dq_parts.append(jnp.concatenate(dq_row, axis=1))
    o_t = jnp.concatenate(o_parts, axis=0).astype(BF16)
    dq = jnp.concatenate(dq_parts, axis=0).T * (HEAD ** -0.5)
    dq = dq * cosine - swap_halves(dq) * sine
    dk = dk * cosine - swap_halves(dk) * sine
    dqkv = jnp.concatenate([dq.astype(BF16), dk.astype(BF16), dv.astype(BF16)], axis=1)
    acc_out[...] += dot(o_t.T, wo)
    acc_dh[...] += dot_t(dqkv, weights)
    dwo = dot(o_t, dy)
    dw = dot(hid_t[...], dqkv)
    dqb = jnp.sum(dqkv.astype(F32), axis=0, keepdims=True)
    if first:
        dwo_ref[...] = dwo
        dqkv_ref[...] = dw
        dqb_ref[...] = dqb
    else:
        dqb_ref[...] = dqb + pqb_ref[...]
        dqkv_buf[...] = dw + pqkv_ref[...]
        dwo_buf[...] = dwo + pwo_ref[...]
        width, cols = dqkv_buf.shape
        steps = pl.num_programs(0)
        part = width // shards // reps
        line = PAIR // reps
        qkv_rows = shards * steps * 3 * part
        for j in range(reps):
            piece = where_ref[0] ^ j
            out = keep_ref.at[j] if j < reps // 2 else give_ref.at[j - reps // 2]
            for zz in range(shards):
                row = (where_ref[1] ^ zz) * (width // shards) + piece * part
                value = dqkv_buf[pl.ds(pl.multiple_of(row, part), part), :].astype(BF16)
                for t in range(3):
                    at = ((zz * steps + step) * 3 + t) * part
                    out[pl.ds(pl.multiple_of(at, part), part), :] = (
                        value[:, t * LANES:(t + 1) * LANES])
            value = dwo_buf[pl.ds(pl.multiple_of(piece * line, line), line), :].astype(BF16)
            for t in range(width // LANES):
                at = qkv_rows + (step * (width // LANES) + t) * line
                out[pl.ds(pl.multiple_of(at, line), line), :] = value[:, t * LANES:(t + 1) * LANES]

    @pl.when(step == pl.num_programs(0) - 1)
    def _():
        rows = send_ref.shape[2]
        width = send_ref.shape[3]
        dh = acc_dh[...]
        send_ref[:, 0] = acc_out[...].astype(BF16).reshape(shards, rows, width)
        send_ref[:, 1] = (dx_ref[...] + dh * gain_ref[...]).astype(BF16).reshape(
            shards, rows, width)
        sums_ref[0:1] = jnp.sum(dh * unit[...], axis=0, keepdims=True)
        sums_ref[1:2] = jnp.sum(dh, axis=0, keepdims=True)
        sums_ref[2:8] = jnp.zeros((6, width), F32)


def attn_call(where, xy, gain, bias, cosine, sine, mask, qkv_bias, weights, wo, partials, previous,
              reps, shards):
    _, _, rows, width = xy.shape
    tokens = shards * rows
    pairs = wo.shape[0] // PAIR
    cols = 3 * PAIR
    first = previous is None
    whole = lambda i, *_: (0, 0)
    in_specs = [
        fixed((shards, 1, rows, width)),
        fixed((shards, 1, rows, width), (0, 1, 0, 0)),
        fixed((1, width)),
        fixed((1, width)),
        fixed((tokens, PAIR)),
        fixed((tokens, PAIR)),
        fixed((tokens, tokens)),
        pl.BlockSpec((1, cols), lambda i, *_: (0, i)),
        pl.BlockSpec((width, cols), lambda i, *_: (0, i)),
        pl.BlockSpec((PAIR, width), lambda i, *_: (i, 0)),
        fixed((tokens, width)),
        fixed((tokens, width)),
    ]
    args = [xy, xy, gain, bias, cosine, sine, mask, qkv_bias, weights, wo, *partials]
    if first:
        grad_shapes = [jax.ShapeDtypeStruct((width, pairs * cols), F32),
                       jax.ShapeDtypeStruct((pairs * PAIR, width), F32)]
        grad_specs = [pl.BlockSpec((width, cols), lambda i, *_: (0, i)),
                      pl.BlockSpec((PAIR, width), lambda i, *_: (i, 0))]
        buffers = []
    else:
        in_specs += [
            pl.BlockSpec((width, cols), lambda i, *_: (0, i)),
            pl.BlockSpec((PAIR, width), lambda i, *_: (i, 0)),
            pl.BlockSpec((1, cols), lambda i, *_: (0, i)),
        ]
        args += list(previous)
        pieces = (reps // 2, width * pairs * (cols + PAIR) // reps // LANES, LANES)
        grad_shapes = [jax.ShapeDtypeStruct(pieces, BF16)] * 2
        grad_specs = [pl.BlockSpec(pieces, lambda i, *_: (0, 0, 0))] * 2
        buffers = [pltpu.VMEM((width, cols), F32), pltpu.VMEM((PAIR, width), F32)]
    return pl.pallas_call(
        partial(attn_kernel, first, reps, shards),
        grid_spec=pltpu.PrefetchScalarGridSpec(
            num_scalar_prefetch=1, grid=(pairs,),
            in_specs=in_specs,
            out_specs=[
            pl.BlockSpec((shards, 2, rows, width), lambda i, *_: (0, 0, 0, 0)),
            *grad_specs,
            pl.BlockSpec((1, cols), lambda i, *_: (0, i)),
            pl.BlockSpec((8, width), whole),
        ],
            scratch_shapes=[
                pltpu.VMEM((tokens, width), BF16),
                pltpu.VMEM((width, tokens), BF16),
                pltpu.VMEM((tokens, width), F32),
                pltpu.VMEM((tokens, width), F32),
                pltpu.VMEM((tokens, width), F32),
                *buffers,
            ]),
        out_shape=[
            jax.ShapeDtypeStruct((shards, 2, rows, width), BF16),
            *grad_shapes,
            jax.ShapeDtypeStruct((1, pairs * cols), F32),
            jax.ShapeDtypeStruct((8, width), F32),
        ],
        compiler_params=pltpu.CompilerParams(
            dimension_semantics=("arbitrary",), vmem_limit_bytes=VMEM_LIMIT),
        cost_estimate=pl.CostEstimate(
            flops=pairs * (6 * tokens * width * 4 * PAIR + 28 * tokens * tokens * PAIR),
            bytes_accessed=20 * 2**20, transcendentals=2 * pairs * tokens * tokens),
    )(where, *args)


def rotation_tables(pos_ids):
    half = ROT // 2
    lane = jnp.arange(PAIR, dtype=jnp.int32) % HEAD
    frequency = 10000.0 ** (-(jnp.arange(half, dtype=F32) * 2.0) / ROT)
    per_lane = jnp.where(lane < ROT, frequency[lane % half], 0.0)
    sign = jnp.where(lane < half, -1.0, jnp.where(lane < ROT, 1.0, 0.0))
    angles = pos_ids.astype(F32)[:, None] * per_lane[None, :]
    return jnp.cos(angles), jnp.sin(angles) * sign[None, :]


def visible_bias(seg_ids, pos_ids, par_ids):
    labels = jnp.arange(par_ids.shape[0], dtype=jnp.int32)
    own = seg_ids[:, None] == labels[None, :]
    parent = jnp.sum(jnp.where(own, par_ids[None, :], 0), axis=1)
    parent_hot = parent[:, None] == labels[None, :]
    grand = jnp.sum(jnp.where(parent_hot, par_ids[None, :], 0), axis=1)
    key_seg = seg_ids[:, None]
    reach = (
        (key_seg == seg_ids[None, :])
        | (key_seg == parent[None, :])
        | (key_seg == grand[None, :])
    )
    return jnp.where(reach & (pos_ids[:, None] <= pos_ids[None, :]), 0.0, NEGATIVE).astype(F32)


def cut_kernel(shards, where_ref, qkv_ref, up_ref, small_ref, *out_refs):
    part, hidden = up_ref.shape
    width = qkv_ref.shape[1] // 3
    slice_d, slice_ff = width // shards, hidden // shards
    for zz in range(shards):
        out = out_refs[zz]
        there = where_ref[1] ^ zz
        at = 0
        for pair in range(slice_d // PAIR):
            for which in range(3):
                col = pl.multiple_of(there * slice_d, LANES) + (which * width + pair * PAIR)
                out[at:at + part, :] = qkv_ref[:, pl.ds(pl.multiple_of(col, LANES), LANES)].astype(BF16)
                at += part
        for tile in range(slice_ff // LANES):
            col = there * slice_ff + tile * LANES
            out[at:at + part, :] = up_ref[:, pl.ds(pl.multiple_of(col, LANES), LANES)].astype(BF16)
            at += part
        out[at:, :] = small_ref[...].astype(BF16)


def cut_call(where, qkv_weight, up_weight, small, reps, shards):
    owned, width3 = qkv_weight.shape
    hidden = up_weight.shape[1]
    part = owned // reps
    lines = (width3 + hidden) // shards // LANES * part + small.shape[0]
    shape = (lines, LANES)
    return pl.pallas_call(
        partial(cut_kernel, shards),
        grid_spec=pltpu.PrefetchScalarGridSpec(
            num_scalar_prefetch=1, grid=(1,),
            in_specs=[
                pl.BlockSpec((part, width3), lambda i, w: (w[0], 0)),
                pl.BlockSpec((part, hidden), lambda i, w: (w[0], 0)),
                pl.BlockSpec(small.shape, lambda i, w: (0, 0)),
            ],
            out_specs=[pl.BlockSpec(shape, lambda i, w: (0, 0))] * shards),
        out_shape=[jax.ShapeDtypeStruct(shape, BF16)] * shards,
    )(where, qkv_weight, up_weight, small)


def join_kernel(shards, where_ref, mine_ref, other_ref, out_ref):
    _, _, part, cols = out_ref.shape
    step = pl.program_id(0)

    def place(ref):
        for zz in range(shards):
            for tile in range(cols // LANES):
                out_ref[where_ref[1] ^ zz, 0, :, tile * LANES:(tile + 1) * LANES] = (
                    ref[0, zz, tile * part:(tile + 1) * part, :])

    @pl.when(step < pl.num_programs(0) // 2)
    def _():
        place(mine_ref)

    @pl.when(step >= pl.num_programs(0) // 2)
    def _():
        place(other_ref)


def halves(reps, block):
    half = reps // 2
    rest = (0,) * (len(block) - 1)
    return [pl.BlockSpec(block, lambda i, w: (jnp.minimum(i, half - 1), *rest)),
            pl.BlockSpec(block, lambda i, w: (jnp.maximum(i - half, 0), *rest))]


def join_call(where, mine, other, part):
    half, shards, lines, _ = mine.shape
    reps = 2 * half
    cols = lines // part * LANES
    out = pl.pallas_call(
        partial(join_kernel, shards),
        grid_spec=pltpu.PrefetchScalarGridSpec(
            num_scalar_prefetch=1, grid=(reps,),
            in_specs=halves(reps, (1, shards, lines, LANES)),
            out_specs=pl.BlockSpec((shards, 1, part, cols), lambda i, w: (0, w[0] ^ i, 0, 0))),
        out_shape=jax.ShapeDtypeStruct((shards, reps, part, cols), BF16),
    )(where, mine, other)
    return out.reshape(shards * reps * part, cols)


def update_kernel(shards, tiles, rates, where_ref, mine_ref, other_ref, *refs):
    *refs, piece = refs
    step = pl.program_id(0)

    @pl.when(step < pl.num_programs(0) // 2)
    def _():
        piece[...] = mine_ref[0]

    @pl.when(step >= pl.num_programs(0) // 2)
    def _():
        piece[...] = other_ref[0]

    def one(weight, moment, average, grad, state, momentum, rate, lines, lead, lane):
        place = (*lead, slice(None), lane)
        g = lines.astype(F32)
        grad[place] = g
        m = MOMENTUM * moment[place] + g
        momentum[place] = m
        w = weight[place] - rate * (g + MOMENTUM * m)
        state[(0, *place)] = w
        state[(1, *place)] = AVERAGE_DECAY * average[place] + (1.0 - AVERAGE_DECAY) * w

    first, second = refs[:3] + refs[6:9], refs[3:6] + refs[9:]
    stride, offsets = tiles
    part = first[0].shape[0]
    at = 0
    for zz in range(shards):
        base = (where_ref[1] ^ zz) * stride
        for offset in offsets:
            lane = pl.ds(pl.multiple_of(base + offset, LANES), LANES)
            one(*first, rates[0], piece[at:at + part, :], (), lane)
            at += part
    count, _, line, width = second[0].shape
    for block in range(count):
        for t in range(width // LANES):
            one(*second, rates[1], piece[at:at + line, :], (block, 0),
                slice(t * LANES, (t + 1) * LANES))
            at += line


def update_call(where, mine, other, first, second, blocks, tiles, rates, shards):
    half, lines, _ = mine.shape
    reps = 2 * half
    owned, cols = first[0].shape
    part = owned // reps
    depth, width = second[0].shape
    line = depth // blocks // reps
    second = [array.reshape(blocks, reps, line, width) for array in second]
    matrix = pl.BlockSpec((part, cols), lambda i, w: (w[0] ^ i, 0))
    quad = pl.BlockSpec((blocks, 1, line, width), lambda i, w: (0, w[0] ^ i, 0, 0))
    outs = pl.pallas_call(
        partial(update_kernel, shards, tiles, rates),
        grid_spec=pltpu.PrefetchScalarGridSpec(
            num_scalar_prefetch=1, grid=(reps,),
            in_specs=halves(reps, (1, lines, LANES)) + [matrix] * 3 + [quad] * 3,
            out_specs=[
                matrix,
                pl.BlockSpec((2, part, cols), lambda i, w: (0, w[0] ^ i, 0)),
                matrix,
                quad,
                pl.BlockSpec((2, blocks, 1, line, width), lambda i, w: (0, 0, w[0] ^ i, 0, 0)),
                quad,
            ],
            scratch_shapes=[pltpu.VMEM((lines, LANES), BF16)]),
        out_shape=[
            jax.ShapeDtypeStruct((owned, cols), F32),
            jax.ShapeDtypeStruct((2, owned, cols), F32),
            jax.ShapeDtypeStruct((owned, cols), F32),
            jax.ShapeDtypeStruct((blocks, reps, line, width), F32),
            jax.ShapeDtypeStruct((2, blocks, reps, line, width), F32),
            jax.ShapeDtypeStruct((blocks, reps, line, width), F32),
        ],
        compiler_params=pltpu.CompilerParams(vmem_limit_bytes=VMEM_LIMIT),
        cost_estimate=pl.CostEstimate(
            flops=8 * (owned * cols + depth * width),
            bytes_accessed=30 * (owned * cols + depth * width), transcendentals=0),
    )(where, mine, other, *first, *second)
    return (outs[:3],
            (outs[3].reshape(depth, width), outs[4].reshape(2, depth, width),
             outs[5].reshape(depth, width)))


def finish_kernel(x_ref, dy_ref, sum_ref, bias_ref, *refs):
    out_ref, grad_ref = refs[-2:]
    x = x_ref[0].astype(F32)
    out_ref[0] = (x + sum_ref[0].astype(F32) + bias_ref[...]).astype(BF16)
    unit, spread = normalize(x)
    scaled = sum_ref[1].astype(F32)
    grad_ref[0] = dy_ref[0].astype(F32) + spread * (
        scaled - jnp.mean(scaled, axis=-1, keepdims=True)
        - unit * jnp.mean(scaled * unit, axis=-1, keepdims=True))


def finish_call(m, block_input, out_cotangent, summed, bias, previous):
    count, rows, width = block_input.shape
    one = pl.BlockSpec((1, rows, width), lambda i: (m, 0, 0))
    in_specs = [one, one, pl.BlockSpec((2, rows, width), lambda i: (0, 0, 0)),
                pl.BlockSpec((1, width), lambda i: (0, 0))]
    in_specs += [pl.BlockSpec(memory_space=pl.ANY)] * len(previous)
    return pl.pallas_call(
        finish_kernel,
        grid=(1,),
        in_specs=in_specs,
        out_specs=[one, one],
        out_shape=[jax.ShapeDtypeStruct((count, rows, width), BF16),
                   jax.ShapeDtypeStruct((count, rows, width), F32)],
        input_output_aliases={4: 0, 5: 1} if previous else {},
    )(block_input, out_cotangent, summed, bias, *previous)


def swap(value, axis, mask):
    size = lax.axis_size(axis)
    return lax.ppermute(value, axis, [(i, i ^ mask) for i in range(size)])


def spread_pieces(piece, half):
    mine = jnp.stack([piece] + [swap(piece, "rep", 2 * k) for k in range(1, half)])
    return mine, swap(mine, "rep", 1)


def sum_pieces(keep, give, half):
    other = swap(give, "rep", 1)
    both = [keep[k].astype(F32) + other[k].astype(F32) for k in range(half)]
    total = both[0]
    for k in range(1, half):
        total = total + swap(both[k].astype(BF16), "rep", 2 * k).astype(F32)
    return total.astype(BF16)


def sum_everywhere(value, half, shards):
    value = value + swap(value, "rep", 1)
    value = sum([swap(value, "rep", 2 * k) for k in range(1, half)], value)
    return sum([swap(value, "shard", k) for k in range(1, shards)], value)


def exchange_columns(piece, lines, shards):
    block = lines // shards
    return jnp.concatenate(
        [piece[:block]]
        + [swap(piece[k * block:(k + 1) * block], "shard", k) for k in range(1, shards)]
        + [piece[lines:]])


def local(
    block_input,
    out_cotangent,
    segment_ids,
    positions,
    parent_ids,
    qkv_weight,
    attn_weight,
    up_weight,
    down_weight,
    small_params,
    qkv_moment,
    attn_moment,
    up_moment,
    down_moment,
    small_moment,
    qkv_average,
    attn_average,
    up_average,
    down_average,
    small_average,
):
    shards = lax.axis_size("shard")
    reps = lax.axis_size("rep")
    half = reps // 2
    rep = lax.axis_index("rep")
    z = lax.axis_index("shard")
    where = jnp.stack([(rep % 2) * half + rep // 2, z]).astype(jnp.int32)
    micro_count, rows, width = block_input.shape
    hidden = up_weight.shape[1]
    part = qkv_weight.shape[0] // reps
    slice_ff = hidden // shards
    slice_d = width // shards
    pairs = slice_d // PAIR
    qkv_cols = 3 * slice_d
    count = small_params.shape[0]

    gathered = [
        lax.all_gather(jnp.stack([block_input[m], out_cotangent[m]]), "shard", axis=0)
        for m in range(micro_count)]

    small_lines = -(-count // (LANES * 16)) * 16
    small = jnp.pad(small_params, (0, small_lines * LANES - count)).reshape(small_lines, LANES)
    messages = cut_call(where, qkv_weight, up_weight, small, reps, shards)
    messages = [messages[0]] + [swap(messages[k], "shard", k) for k in range(1, shards)]
    lines = messages[0].shape[0] - small_lines
    piece = jnp.stack([message[:lines] for message in messages])
    weights = join_call(where, *spread_pieces(piece, half), part)
    small_all = jnp.stack([message[lines:].reshape(-1)[:count] for message in messages])
    small_full = small_all[z ^ jnp.arange(shards)].reshape(-1).astype(F32)
    down_bf = down_weight.astype(BF16)
    attn_bf = attn_weight.astype(BF16)

    gain_one, bias_one, gain_two, bias_two = (
        small_full[i * width:(i + 1) * width].reshape(1, width) for i in range(4))
    qkv_bias = small_full[4 * width:7 * width].reshape(3, shards, pairs, PAIR)
    qkv_bias = lax.dynamic_index_in_dim(qkv_bias, z, 1, keepdims=False)
    qkv_bias = qkv_bias.transpose(1, 0, 2).reshape(1, qkv_cols)
    attn_bias = small_full[7 * width:8 * width]
    up_bias = lax.dynamic_slice_in_dim(
        small_full[8 * width:8 * width + hidden], z * slice_ff, slice_ff, 0).reshape(1, slice_ff)
    down_bias = small_full[8 * width + hidden:]
    out_bias = (attn_bias + down_bias).reshape(1, width)

    mlp_previous = None
    attn_previous = None
    sums_two = 0.0
    sums_one = 0.0
    summed = []
    for m in range(micro_count):
        xy = gathered[m]
        cosine, sine = rotation_tables(positions[m])
        mask = visible_bias(segment_ids[m], positions[m], parent_ids[m, 0])
        out_part, dx_part, *mlp_previous, sums = mlp_call(
            where, xy, gain_two, bias_two, up_bias, weights, down_bf, mlp_previous, reps, shards,
            qkv_cols)
        sums_two = sums_two + sums
        send, *attn_previous, sums = attn_call(
            where, xy, gain_one, bias_one, cosine, sine, mask, qkv_bias, weights, attn_bf,
            (out_part, dx_part), attn_previous, reps, shards)
        sums_one = sums_one + sums
        summed.append(lax.psum_scatter(send, "shard", scatter_dimension=0, tiled=False))

    all_tok = micro_count * rows * shards * reps
    rates = [rate / math.sqrt(all_tok) for rate in RATES]
    mlp_keep, mlp_give, grad_up_bias = mlp_previous
    attn_keep, attn_give, grad_qkv_bias = attn_previous

    piece = sum_pieces(mlp_keep, mlp_give, half)
    piece = exchange_columns(piece, width * slice_ff // reps // LANES, shards)
    mine, other = spread_pieces(piece, half)
    blocks = slice_ff // (256 if slice_ff % 256 == 0 and qkv_cols % 256 == 0 else 128)
    up_new, down_new = update_call(
        where, mine, other, (up_weight, up_moment, up_average),
        (down_weight, down_moment, down_average), blocks,
        (slice_ff, range(0, slice_ff, LANES)), (rates[2], rates[3]), shards)

    piece = sum_pieces(attn_keep, attn_give, half)
    piece = exchange_columns(piece, width * qkv_cols // reps // LANES, shards)
    mine, other = spread_pieces(piece, half)
    offsets = [which * width + pair * PAIR for pair in range(pairs) for which in range(3)]
    qkv_new, attn_new = update_call(
        where, mine, other, (qkv_weight, qkv_moment, qkv_average),
        (attn_weight, attn_moment, attn_average), pairs, (slice_d, offsets),
        (rates[0], rates[1]), shards)

    head_part = jnp.concatenate(
        [sums_one[0], sums_one[1], sums_two[0], sums_two[1]])
    bias_part = lax.dynamic_update_slice(
        jnp.zeros((3, shards, slice_d), F32),
        grad_qkv_bias.reshape(pairs, 3, PAIR).transpose(1, 0, 2).reshape(3, 1, slice_d),
        (0, z, 0)).reshape(-1)
    token_part = jnp.where(z == 0, sums_two[2], 0.0)
    ff_part = lax.dynamic_update_slice(
        jnp.zeros((hidden,), F32), grad_up_bias.reshape(-1), (z * slice_ff,))
    small_grad = jnp.concatenate([head_part, bias_part, token_part, ff_part, token_part])
    small_grad = sum_everywhere(small_grad.reshape(-1, LANES), half, shards).reshape(-1)
    small_grad = lax.dynamic_slice_in_dim(small_grad, z * count, count, 0)
    small_momentum = MOMENTUM * small_moment + small_grad
    small_weight = small_params - rates[4] * (small_grad + MOMENTUM * small_momentum)
    small_mean = AVERAGE_DECAY * small_average + (1.0 - AVERAGE_DECAY) * small_weight

    results = ()
    for m in range(micro_count):
        results = finish_call(m, block_input, out_cotangent, summed[m], out_bias, results)

    updated = (qkv_new, attn_new, up_new, down_new,
               (small_grad, jnp.stack([small_weight, small_mean]), small_momentum))
    return (*results, *(new[0] for new in updated), *(new[1] for new in updated),
            *(new[2] for new in updated))


def solution(mesh):
    tokens = P(None, ("rep", "shard"), None)
    tree = P(None, "rep")
    matrix = P("shard", None)
    vector = P("shard")
    weights = (matrix, matrix, matrix, matrix, vector)
    state = P(None, "shard", None)
    return jax.shard_map(
        local,
        mesh=mesh,
        in_specs=(tokens, tokens, tree, tree, P(None, "rep", None), *weights, *weights, *weights),
        out_specs=(tokens, tokens, *weights, state, state, state, state, P(None, "shard"),
                   *weights),
        check_vma=False,
    )
```

```python
from functools import partial
import math

import jax
import jax.numpy as jnp
import numpy as np
from jax import lax
from jax.experimental import pallas as pl
from jax.experimental.pallas import tpu as pltpu
from jax.sharding import PartitionSpec as P

HEAD = 64
ROT = 16
PAIR = 2 * HEAD
LANES = 128

EPSILON = 1e-05
NEGATIVE = -1e30
MOMENTUM = 0.5
AVERAGE_DECAY = 0.5
RATES = (0.045, 0.8, 0.1, 0.024, 0.4)

F32 = jnp.float32
BF16 = jnp.bfloat16
VMEM_LIMIT = 60 * 1024 * 1024


def dot(a, b):
    return jnp.dot(a, b, preferred_element_type=F32)


def dot_t(a, b):
    return lax.dot_general(a, b, (((1,), (1,)), ((), ())), preferred_element_type=F32)


def normalize(values):
    center = values - jnp.mean(values, axis=-1, keepdims=True)
    spread = lax.rsqrt(jnp.mean(center * center, axis=-1, keepdims=True) + EPSILON)
    return center * spread, spread


def fixed(shape, index=None):
    zeros = (0,) * len(shape) if index is None else index
    return pl.BlockSpec(shape, lambda *_: zeros, pipeline_mode=pl.Buffered(1))


def rows_of(ref):
    block = ref[...]
    return block.reshape(-1, block.shape[-1])


def mlp_kernel(first, reps, shards, where_ref, *refs):
    if first:
        (x_ref, dy_ref, gain_ref, bias_ref, ub_ref, up_ref, down_ref,
         out_ref, dx_ref, dup_ref, ddown_ref, dub_ref, sums_ref,
         hid, hid_t, unit, acc_out, acc_dx) = refs
    else:
        (x_ref, dy_ref, gain_ref, bias_ref, ub_ref, up_ref, down_ref, pup_ref, pdown_ref, pub_ref,
         out_ref, dx_ref, keep_ref, give_ref, dub_ref, sums_ref,
         hid, hid_t, unit, acc_out, acc_dx, dup_buf, ddown_buf) = refs
    step = pl.program_id(0)

    @pl.when(step == 0)
    def _():
        xhat, _ = normalize(rows_of(x_ref).astype(F32))
        unit[...] = xhat
        h = (xhat * gain_ref[...] + bias_ref[...]).astype(BF16)
        hid[...] = h
        hid_t[...] = h.T
        acc_out[...] = jnp.zeros_like(acc_out)
        acc_dx[...] = jnp.zeros_like(acc_dx)

    dy = rows_of(dy_ref)
    up = up_ref[...]
    down = down_ref[...]
    u = dot(hid[...], up) + ub_ref[...]
    cdf = 0.5 * (1.0 + lax.erf(u * (0.5 ** 0.5)))
    act = (u * cdf).astype(BF16)
    slope = cdf + u * (jnp.exp(-0.5 * u * u) * ((2.0 * math.pi) ** -0.5))
    dact = dot_t(dy, down)
    du32 = dact * slope
    du = du32.astype(BF16)
    acc_out[...] += dot(act, down)
    acc_dx[...] += dot_t(du, up)
    ddown = dot(act.T, dy)
    dup = dot(hid_t[...], du)
    dub = jnp.sum(du.astype(F32), axis=0, keepdims=True)
    if first:
        ddown_ref[...] = ddown
        dub_ref[...] = dub
        dup_ref[...] = dup
    else:
        dub_ref[...] = dub + pub_ref[...]
        dup_buf[...] = dup + pup_ref[...]
        ddown_buf[...] = ddown + pdown_ref[...]
        width, block = dup_buf.shape
        steps = pl.num_programs(0)
        part = width // shards // reps
        tiles = block // LANES
        line = block // reps
        up_rows = shards * steps * tiles * part
        for j in range(reps):
            piece = where_ref[0] ^ j
            out = keep_ref.at[j] if j < reps // 2 else give_ref.at[j - reps // 2]
            for zz in range(shards):
                row = (where_ref[1] ^ zz) * (width // shards) + piece * part
                value = dup_buf[pl.ds(pl.multiple_of(row, part), part), :].astype(BF16)
                for t in range(tiles):
                    at = ((zz * steps + step) * tiles + t) * part
                    out[pl.ds(pl.multiple_of(at, part), part), :] = (
                        value[:, t * LANES:(t + 1) * LANES])
            value = ddown_buf[pl.ds(pl.multiple_of(piece * line, line), line), :].astype(BF16)
            for t in range(width // LANES):
                at = up_rows + (step * (width // LANES) + t) * line
                out[pl.ds(pl.multiple_of(at, line), line), :] = value[:, t * LANES:(t + 1) * LANES]

    @pl.when(step == pl.num_programs(0) - 1)
    def _():
        dh = acc_dx[...]
        out_ref[...] = acc_out[...]
        dx_ref[...] = dh * gain_ref[...]
        sums_ref[0:1] = jnp.sum(dh * unit[...], axis=0, keepdims=True)
        sums_ref[1:2] = jnp.sum(dh, axis=0, keepdims=True)
        sums_ref[2:3] = jnp.sum(dy.astype(F32), axis=0, keepdims=True)
        sums_ref[3:8] = jnp.zeros((5, dh.shape[1]), F32)


def mlp_call(where, xy, gain, bias, up_bias, weights, down, previous, reps, shards, first_col):
    _, _, rows, width = xy.shape
    tokens = shards * rows
    hidden = down.shape[0]
    block = 256 if hidden % 256 == 0 and first_col % 256 == 0 else 128
    steps = hidden // block
    offset = first_col // block
    first = previous is None
    whole = lambda i, *_: (0, 0)
    in_specs = [
        fixed((shards, 1, rows, width)),
        fixed((shards, 1, rows, width), (0, 1, 0, 0)),
        fixed((1, width)),
        fixed((1, width)),
        pl.BlockSpec((1, block), lambda i, *_: (0, i)),
        pl.BlockSpec((width, block), lambda i, *_: (0, offset + i)),
        pl.BlockSpec((block, width), lambda i, *_: (i, 0)),
    ]
    args = [xy, xy, gain, bias, up_bias, weights, down]
    if first:
        grad_shapes = [jax.ShapeDtypeStruct((width, hidden), F32),
                       jax.ShapeDtypeStruct((hidden, width), F32)]
        grad_specs = [pl.BlockSpec((width, block), lambda i, *_: (0, i)),
                      pl.BlockSpec((block, width), lambda i, *_: (i, 0))]
        buffers = []
    else:
        in_specs += [
            pl.BlockSpec((width, block), lambda i, *_: (0, i)),
            pl.BlockSpec((block, width), lambda i, *_: (i, 0)),
            pl.BlockSpec((1, block), lambda i, *_: (0, i)),
        ]
        args += list(previous)
        pieces = (reps // 2, 2 * width * hidden // reps // LANES, LANES)
        grad_shapes = [jax.ShapeDtypeStruct(pieces, BF16)] * 2
        grad_specs = [pl.BlockSpec(pieces, lambda i, *_: (0, 0, 0))] * 2
        buffers = [pltpu.VMEM((width, block), F32), pltpu.VMEM((block, width), F32)]
    return pl.pallas_call(
        partial(mlp_kernel, first, reps, shards),
        grid_spec=pltpu.PrefetchScalarGridSpec(
            num_scalar_prefetch=1, grid=(steps,),
            in_specs=in_specs,
            out_specs=[
            pl.BlockSpec((tokens, width), whole),
            pl.BlockSpec((tokens, width), whole),
            *grad_specs,
            pl.BlockSpec((1, block), lambda i, *_: (0, i)),
            pl.BlockSpec((8, width), whole),
        ],
            scratch_shapes=[
                pltpu.VMEM((tokens, width), BF16),
                pltpu.VMEM((width, tokens), BF16),
                pltpu.VMEM((tokens, width), F32),
                pltpu.VMEM((tokens, width), F32),
                pltpu.VMEM((tokens, width), F32),
                *buffers,
            ]),
        out_shape=[
            jax.ShapeDtypeStruct((tokens, width), F32),
            jax.ShapeDtypeStruct((tokens, width), F32),
            *grad_shapes,
            jax.ShapeDtypeStruct((1, hidden), F32),
            jax.ShapeDtypeStruct((8, width), F32),
        ],
        compiler_params=pltpu.CompilerParams(
            dimension_semantics=("arbitrary",), vmem_limit_bytes=VMEM_LIMIT),
        cost_estimate=pl.CostEstimate(
            flops=12 * tokens * width * hidden, bytes_accessed=24 * 2**20,
            transcendentals=2 * tokens * hidden),
    )(where, *args)


def swap_halves(values):
    half = ROT // 2
    lane = lax.broadcasted_iota(jnp.int32, values.shape, 1) % HEAD
    return jnp.where(lane < half, pltpu.roll(values, PAIR - half, 1), pltpu.roll(values, half, 1))


def attn_kernel(first, reps, shards, where_ref, *refs):
    if first:
        (x_ref, dy_ref, gain_ref, bias_ref, cos_ref, sin_ref, mask_ref, qb_ref, qkv_ref, wo_ref,
         out_ref, dx_ref,
         send_ref, dqkv_ref, dwo_ref, dqb_ref, sums_ref,
         hid, hid_t, unit, acc_out, acc_dh) = refs
    else:
        (x_ref, dy_ref, gain_ref, bias_ref, cos_ref, sin_ref, mask_ref, qb_ref, qkv_ref, wo_ref,
         out_ref, dx_ref, pqkv_ref, pwo_ref, pqb_ref,
         send_ref, keep_ref, give_ref, dqb_ref, sums_ref,
         hid, hid_t, unit, acc_out, acc_dh, dqkv_buf, dwo_buf) = refs
    step = pl.program_id(0)

    @pl.when(step == 0)
    def _():
        xhat, _ = normalize(rows_of(x_ref).astype(F32))
        unit[...] = xhat
        h = (xhat * gain_ref[...] + bias_ref[...]).astype(BF16)
        hid[...] = h
        hid_t[...] = h.T
        acc_out[...] = out_ref[...]
        acc_dh[...] = jnp.zeros_like(acc_dh)

    dy = rows_of(dy_ref)
    weights = qkv_ref[...]
    wo = wo_ref[...]
    cosine = cos_ref[...]
    sine = sin_ref[...]
    lin = dot(hid[...], weights) + qb_ref[...]
    q32 = lin[:, :PAIR]
    k32 = lin[:, PAIR:2 * PAIR]
    q = (q32 * cosine + swap_halves(q32) * sine).astype(BF16) * BF16(HEAD ** -0.5)
    k = (k32 * cosine + swap_halves(k32) * sine).astype(BF16)
    v = lin[:, 2 * PAIR:].astype(BF16)
    do = dot_t(dy, wo).astype(BF16)
    k_t = k.T
    v_t = v.T
    lane = lax.broadcasted_iota(jnp.int32, q.shape, 1)
    o_parts = []
    dq_parts = []
    dk = None
    dv = None
    tokens = q.shape[0]
    chunk = tokens if tokens <= 640 else tokens // 2
    for head in range(2):
        own = (lane // HEAD) == head
        q_h = jnp.where(own, q, jnp.zeros_like(q))
        do_h = jnp.where(own, do, jnp.zeros_like(do))
        part = slice(head * HEAD, (head + 1) * HEAD)
        o_row = []
        dq_row = []
        for at in range(0, tokens, chunk):
            q_c = q_h[at:at + chunk]
            do_c = do_h[at:at + chunk]
            scores = dot_t(k, q_c) + mask_ref[:, at:at + chunk]
            top = jnp.max(scores, axis=0, keepdims=True)
            e = jnp.exp(scores - top)
            prob = e * (1.0 / jnp.sum(e, axis=0, keepdims=True))
            prob_bf = prob.astype(BF16)
            o_row.append(dot(v_t[part], prob_bf))
            dprob = dot_t(v, do_c)
            weighted = prob * dprob
            delta = jnp.sum(weighted, axis=0, keepdims=True)
            ds = (weighted - prob * delta).astype(BF16)
            dq_row.append(dot(k_t[part], ds))
            dk_c = dot(ds, q_c)
            dv_c = dot(prob_bf, do_c)
            dk = dk_c if dk is None else dk + dk_c
            dv = dv_c if dv is None else dv + dv_c
        o_parts.append(jnp.concatenate(o_row, axis=1))
        dq_parts.append(jnp.concatenate(dq_row, axis=1))
    o_t = jnp.concatenate(o_parts, axis=0).astype(BF16)
    dq = jnp.concatenate(dq_parts, axis=0).T * (HEAD ** -0.5)
    dq = dq * cosine - swap_halves(dq) * sine
    dk = dk * cosine - swap_halves(dk) * sine
    dqkv = jnp.concatenate([dq.astype(BF16), dk.astype(BF16), dv.astype(BF16)], axis=1)
    acc_out[...] += dot(o_t.T, wo)
    acc_dh[...] += dot_t(dqkv, weights)
    dwo = dot(o_t, dy)
    dw = dot(hid_t[...], dqkv)
    dqb = jnp.sum(dqkv.astype(F32), axis=0, keepdims=True)
    if first:
        dwo_ref[...] = dwo
        dqkv_ref[...] = dw
        dqb_ref[...] = dqb
    else:
        dqb_ref[...] = dqb + pqb_ref[...]
        dqkv_buf[...] = dw + pqkv_ref[...]
        dwo_buf[...] = dwo + pwo_ref[...]
        width, cols = dqkv_buf.shape
        steps = pl.num_programs(0)
        part = width // shards // reps
        line = PAIR // reps
        qkv_rows = shards * steps * 3 * part
        for j in range(reps):
            piece = where_ref[0] ^ j
            out = keep_ref.at[j] if j < reps // 2 else give_ref.at[j - reps // 2]
            for zz in range(shards):
                row = (where_ref[1] ^ zz) * (width // shards) + piece * part
                value = dqkv_buf[pl.ds(pl.multiple_of(row, part), part), :].astype(BF16)
                for t in range(3):
                    at = ((zz * steps + step) * 3 + t) * part
                    out[pl.ds(pl.multiple_of(at, part), part), :] = (
                        value[:, t * LANES:(t + 1) * LANES])
            value = dwo_buf[pl.ds(pl.multiple_of(piece * line, line), line), :].astype(BF16)
            for t in range(width // LANES):
                at = qkv_rows + (step * (width // LANES) + t) * line
                out[pl.ds(pl.multiple_of(at, line), line), :] = value[:, t * LANES:(t + 1) * LANES]

    @pl.when(step == pl.num_programs(0) - 1)
    def _():
        rows = send_ref.shape[2]
        width = send_ref.shape[3]
        dh = acc_dh[...]
        send_ref[:, 0] = acc_out[...].astype(BF16).reshape(shards, rows, width)
        send_ref[:, 1] = (dx_ref[...] + dh * gain_ref[...]).astype(BF16).reshape(
            shards, rows, width)
        sums_ref[0:1] = jnp.sum(dh * unit[...], axis=0, keepdims=True)
        sums_ref[1:2] = jnp.sum(dh, axis=0, keepdims=True)
        sums_ref[2:8] = jnp.zeros((6, width), F32)


def attn_call(where, xy, gain, bias, cosine, sine, mask, qkv_bias, weights, wo, partials, previous,
              reps, shards):
    _, _, rows, width = xy.shape
    tokens = shards * rows
    pairs = wo.shape[0] // PAIR
    cols = 3 * PAIR
    first = previous is None
    whole = lambda i, *_: (0, 0)
    in_specs = [
        fixed((shards, 1, rows, width)),
        fixed((shards, 1, rows, width), (0, 1, 0, 0)),
        fixed((1, width)),
        fixed((1, width)),
        fixed((tokens, PAIR)),
        fixed((tokens, PAIR)),
        fixed((tokens, tokens)),
        pl.BlockSpec((1, cols), lambda i, *_: (0, i)),
        pl.BlockSpec((width, cols), lambda i, *_: (0, i)),
        pl.BlockSpec((PAIR, width), lambda i, *_: (i, 0)),
        fixed((tokens, width)),
        fixed((tokens, width)),
    ]
    args = [xy, xy, gain, bias, cosine, sine, mask, qkv_bias, weights, wo, *partials]
    if first:
        grad_shapes = [jax.ShapeDtypeStruct((width, pairs * cols), F32),
                       jax.ShapeDtypeStruct((pairs * PAIR, width), F32)]
        grad_specs = [pl.BlockSpec((width, cols), lambda i, *_: (0, i)),
                      pl.BlockSpec((PAIR, width), lambda i, *_: (i, 0))]
        buffers = []
    else:
        in_specs += [
            pl.BlockSpec((width, cols), lambda i, *_: (0, i)),
            pl.BlockSpec((PAIR, width), lambda i, *_: (i, 0)),
            pl.BlockSpec((1, cols), lambda i, *_: (0, i)),
        ]
        args += list(previous)
        pieces = (reps // 2, width * pairs * (cols + PAIR) // reps // LANES, LANES)
        grad_shapes = [jax.ShapeDtypeStruct(pieces, BF16)] * 2
        grad_specs = [pl.BlockSpec(pieces, lambda i, *_: (0, 0, 0))] * 2
        buffers = [pltpu.VMEM((width, cols), F32), pltpu.VMEM((PAIR, width), F32)]
    return pl.pallas_call(
        partial(attn_kernel, first, reps, shards),
        grid_spec=pltpu.PrefetchScalarGridSpec(
            num_scalar_prefetch=1, grid=(pairs,),
            in_specs=in_specs,
            out_specs=[
            pl.BlockSpec((shards, 2, rows, width), lambda i, *_: (0, 0, 0, 0)),
            *grad_specs,
            pl.BlockSpec((1, cols), lambda i, *_: (0, i)),
            pl.BlockSpec((8, width), whole),
        ],
            scratch_shapes=[
                pltpu.VMEM((tokens, width), BF16),
                pltpu.VMEM((width, tokens), BF16),
                pltpu.VMEM((tokens, width), F32),
                pltpu.VMEM((tokens, width), F32),
                pltpu.VMEM((tokens, width), F32),
                *buffers,
            ]),
        out_shape=[
            jax.ShapeDtypeStruct((shards, 2, rows, width), BF16),
            *grad_shapes,
            jax.ShapeDtypeStruct((1, pairs * cols), F32),
            jax.ShapeDtypeStruct((8, width), F32),
        ],
        compiler_params=pltpu.CompilerParams(
            dimension_semantics=("arbitrary",), vmem_limit_bytes=VMEM_LIMIT),
        cost_estimate=pl.CostEstimate(
            flops=pairs * (6 * tokens * width * 4 * PAIR + 28 * tokens * tokens * PAIR),
            bytes_accessed=20 * 2**20, transcendentals=2 * pairs * tokens * tokens),
    )(where, *args)


def rotation_tables(pos_ids):
    half = ROT // 2
    lane = np.arange(PAIR) % HEAD
    frequency = 10000.0 ** (-(lane % half * 2.0) / ROT)
    per_lane = np.where(lane < ROT, frequency, 0.0).astype(np.float32)
    sign = np.where(lane < half, -1.0, np.where(lane < ROT, 1.0, 0.0)).astype(np.float32)
    angles = pos_ids.astype(F32)[:, None] * per_lane[None, :]
    return jnp.cos(angles), jnp.sin(angles) * sign[None, :]


def visible_bias(seg_ids, pos_ids, par_ids):
    labels = jnp.arange(par_ids.shape[0], dtype=jnp.int32)
    own = seg_ids[:, None] == labels[None, :]
    parent = jnp.sum(jnp.where(own, par_ids[None, :], 0), axis=1)
    parent_hot = parent[:, None] == labels[None, :]
    grand = jnp.sum(jnp.where(parent_hot, par_ids[None, :], 0), axis=1)
    key_seg = seg_ids[:, None]
    reach = (
        (key_seg == seg_ids[None, :])
        | (key_seg == parent[None, :])
        | (key_seg == grand[None, :])
    )
    return jnp.where(reach & (pos_ids[:, None] <= pos_ids[None, :]), 0.0, NEGATIVE).astype(F32)


def cut_kernel(shards, where_ref, qkv_ref, up_ref, small_ref, *out_refs):
    part, hidden = up_ref.shape
    width = qkv_ref.shape[1] // 3
    slice_d, slice_ff = width // shards, hidden // shards
    for zz in range(shards):
        out = out_refs[zz]
        there = where_ref[1] ^ zz
        at = 0
        for pair in range(slice_d // PAIR):
            for which in range(3):
                col = pl.multiple_of(there * slice_d, LANES) + (which * width + pair * PAIR)
                out[at:at + part, :] = qkv_ref[:, pl.ds(pl.multiple_of(col, LANES), LANES)].astype(BF16)
                at += part
        for tile in range(slice_ff // LANES):
            col = there * slice_ff + tile * LANES
            out[at:at + part, :] = up_ref[:, pl.ds(pl.multiple_of(col, LANES), LANES)].astype(BF16)
            at += part
        out[at:, :] = small_ref[...].astype(BF16)


def cut_call(where, qkv_weight, up_weight, small, reps, shards):
    owned, width3 = qkv_weight.shape
    hidden = up_weight.shape[1]
    part = owned // reps
    lines = (width3 + hidden) // shards // LANES * part + small.shape[0]
    shape = (lines, LANES)
    return pl.pallas_call(
        partial(cut_kernel, shards),
        grid_spec=pltpu.PrefetchScalarGridSpec(
            num_scalar_prefetch=1, grid=(1,),
            in_specs=[
                pl.BlockSpec((part, width3), lambda i, w: (w[0], 0)),
                pl.BlockSpec((part, hidden), lambda i, w: (w[0], 0)),
                pl.BlockSpec(small.shape, lambda i, w: (0, 0)),
            ],
            out_specs=[pl.BlockSpec(shape, lambda i, w: (0, 0))] * shards),
        out_shape=[jax.ShapeDtypeStruct(shape, BF16)] * shards,
    )(where, qkv_weight, up_weight, small)


def join_kernel(shards, where_ref, ref, out_ref):
    half, _, lines, _ = ref.shape
    _, _, part, cols = out_ref.shape
    for k in range(half):
        for zz in range(shards):
            for tile in range(cols // LANES):
                out_ref[where_ref[1] ^ zz, (where_ref[0] % half) ^ k, :,
                        tile * LANES:(tile + 1) * LANES] = (
                    ref[k, zz, tile * part:(tile + 1) * part, :])


def join_call(where, pieces, previous, part):
    half, shards, lines, _ = pieces.shape
    cols = lines // part * LANES
    other = len(previous)
    core = lambda w: (w[0] // half) ^ other

    def body(where_ref, ref, *refs):
        join_kernel(shards, where_ref, ref, refs[-1])

    return pl.pallas_call(
        body,
        grid_spec=pltpu.PrefetchScalarGridSpec(
            num_scalar_prefetch=1, grid=(1,),
            in_specs=[pl.BlockSpec(pieces.shape, lambda i, w: (0, 0, 0, 0))]
            + [pl.BlockSpec(memory_space=pl.ANY)] * other,
            out_specs=pl.BlockSpec((shards, half, part, cols), lambda i, w: (0, core(w), 0, 0))),
        out_shape=jax.ShapeDtypeStruct((shards, 2 * half, part, cols), BF16),
        input_output_aliases={2: 0} if other else {},
        compiler_params=pltpu.CompilerParams(vmem_limit_bytes=VMEM_LIMIT),
    )(where, pieces, *previous)


def update_kernel(shards, tiles, rates, where_ref, piece, *refs):
    *refs, token_ref = refs
    token_ref[...] = jnp.zeros_like(token_ref)
    refs = refs[:6] + refs[-6:]

    def one(weight, moment, average, grad, state, momentum, rate, lines, lead, lane):
        place = (*lead, slice(None), lane)
        g = lines.astype(F32)
        grad[place] = g
        m = MOMENTUM * moment[place] + g
        momentum[place] = m
        w = weight[place] - rate * (g + MOMENTUM * m)
        state[(0, *place)] = w
        state[(1, *place)] = AVERAGE_DECAY * average[place] + (1.0 - AVERAGE_DECAY) * w

    first, second = refs[:3] + refs[6:9], refs[3:6] + refs[9:]
    stride, offsets = tiles
    part = first[0].shape[0]
    at = 0
    for zz in range(shards):
        base = (where_ref[1] ^ zz) * stride
        for offset in offsets:
            lane = pl.ds(pl.multiple_of(base + offset, LANES), LANES)
            one(*first, rates[0], piece[0, at:at + part, :], (), lane)
            at += part
    count, _, line, width = second[0].shape
    for block in range(count):
        for t in range(width // LANES):
            one(*second, rates[1], piece[0, at:at + line, :], (block, 0),
                slice(t * LANES, (t + 1) * LANES))
            at += line


def update_half(where, pieces, first, second, previous, after, blocks, tiles, rates, shards):
    half, lines, _ = pieces.shape
    reps = 2 * half
    owned, cols = first[0].shape
    part = owned // reps
    _, _, line, width = second[0].shape
    skip = half if previous else 0
    matrix = pl.BlockSpec((part, cols), lambda i, w: (w[0] ^ (i + skip), 0))
    quad = pl.BlockSpec((blocks, 1, line, width), lambda i, w: (0, w[0] ^ (i + skip), 0, 0))
    return pl.pallas_call(
        partial(update_kernel, shards, tiles, rates),
        grid_spec=pltpu.PrefetchScalarGridSpec(
            num_scalar_prefetch=1, grid=(half,),
            in_specs=[pl.BlockSpec((1, lines, LANES), lambda i, w: (i, 0, 0))]
            + [matrix] * 3 + [quad] * 3 + [pl.BlockSpec(memory_space=pl.ANY)] * (len(previous) + len(after)),
            out_specs=[
                matrix,
                pl.BlockSpec((2, part, cols), lambda i, w: (0, w[0] ^ (i + skip), 0)),
                matrix,
                quad,
                pl.BlockSpec((2, blocks, 1, line, width),
                             lambda i, w: (0, 0, w[0] ^ (i + skip), 0, 0)),
                quad,
                pl.BlockSpec((8, LANES), lambda i, w: (0, 0)),
            ]),
        out_shape=[
            jax.ShapeDtypeStruct((owned, cols), F32),
            jax.ShapeDtypeStruct((2, owned, cols), F32),
            jax.ShapeDtypeStruct((owned, cols), F32),
            jax.ShapeDtypeStruct((blocks, reps, line, width), F32),
            jax.ShapeDtypeStruct((2, blocks, reps, line, width), F32),
            jax.ShapeDtypeStruct((blocks, reps, line, width), F32),
            jax.ShapeDtypeStruct((8, LANES), F32),
        ],
        input_output_aliases={8 + i: i for i in range(len(previous))},
        compiler_params=pltpu.CompilerParams(vmem_limit_bytes=VMEM_LIMIT),
        cost_estimate=pl.CostEstimate(
            flops=4 * reps * (part * cols + blocks * line * width),
            bytes_accessed=14 * reps * (part * cols + blocks * line * width), transcendentals=0),
    )(where, pieces, *first, *second, *previous, *after)


def update_call(where, mine, other, first, second, after, blocks, tiles, rates, shards):
    depth, width = second[0].shape
    reps = 2 * mine.shape[0]
    second = [array.reshape(blocks, reps, depth // blocks // reps, width) for array in second]
    early = update_half(where, mine, first, second, [], after, blocks, tiles, rates, shards)
    outs = update_half(where, other, first, second, early[:6], [], blocks, tiles, rates, shards)
    return (outs[:3],
            (outs[3].reshape(depth, width), outs[4].reshape(2, depth, width),
             outs[5].reshape(depth, width)), early[6], outs[6])


def finish_kernel(x_ref, dy_ref, sum_ref, bias_ref, *refs):
    out_ref, grad_ref = refs[-2:]
    x = x_ref[0].astype(F32)
    out_ref[0] = (x + sum_ref[0].astype(F32) + bias_ref[...]).astype(BF16)
    unit, spread = normalize(x)
    scaled = sum_ref[1].astype(F32)
    grad_ref[0] = dy_ref[0].astype(F32) + spread * (
        scaled - jnp.mean(scaled, axis=-1, keepdims=True)
        - unit * jnp.mean(scaled * unit, axis=-1, keepdims=True))


def finish_call(m, block_input, out_cotangent, summed, bias, previous):
    count, rows, width = block_input.shape
    one = pl.BlockSpec((1, rows, width), lambda i: (m, 0, 0))
    in_specs = [one, one, pl.BlockSpec((2, rows, width), lambda i: (0, 0, 0)),
                pl.BlockSpec((1, width), lambda i: (0, 0))]
    in_specs += [pl.BlockSpec(memory_space=pl.ANY)] * len(previous)
    return pl.pallas_call(
        finish_kernel,
        grid=(1,),
        in_specs=in_specs,
        out_specs=[one, one],
        out_shape=[jax.ShapeDtypeStruct((count, rows, width), BF16),
                   jax.ShapeDtypeStruct((count, rows, width), F32)],
        input_output_aliases={4: 0, 5: 1} if previous else {},
    )(block_input, out_cotangent, summed, bias, *previous)


def swap(value, axis, mask):
    size = lax.axis_size(axis)
    return lax.ppermute(value, axis, [(i, i ^ mask) for i in range(size)])


def tie(*values):
    return lax.optimization_barrier(values)


def spread_chips(piece, half):
    return jnp.stack([piece] + [swap(piece, "rep", 2 * k) for k in range(1, half)])


def spread_pieces(piece, half):
    mine = spread_chips(piece, half)
    return mine, swap(mine, "rep", 1)


def sum_cores(keep, give, half):
    other = swap(give, "rep", 1)
    both = [keep[k].astype(F32) + other[k].astype(F32) for k in range(half)]
    return both[:1] + [value.astype(BF16) for value in both[1:]]


def sum_chips(both, half):
    total = both[0]
    for k in range(1, half):
        total = total + swap(both[k], "rep", 2 * k).astype(F32)
    return total.astype(BF16)


def exchange_columns(piece, lines, shards):
    block = lines // shards
    return jnp.concatenate(
        [piece[:block]]
        + [swap(piece[k * block:(k + 1) * block], "shard", k) for k in range(1, shards)]
        + [piece[lines:]])


def local(
    block_input,
    out_cotangent,
    segment_ids,
    positions,
    parent_ids,
    qkv_weight,
    attn_weight,
    up_weight,
    down_weight,
    small_params,
    qkv_moment,
    attn_moment,
    up_moment,
    down_moment,
    small_moment,
    qkv_average,
    attn_average,
    up_average,
    down_average,
    small_average,
):
    shards = lax.axis_size("shard")
    reps = lax.axis_size("rep")
    half = reps // 2
    rep = lax.axis_index("rep")
    z = lax.axis_index("shard")
    where = jnp.stack([(rep % 2) * half + rep // 2, z]).astype(jnp.int32)
    micro_count, rows, width = block_input.shape
    hidden = up_weight.shape[1]
    part = qkv_weight.shape[0] // reps
    slice_ff = hidden // shards
    slice_d = width // shards
    pairs = slice_d // PAIR
    qkv_cols = 3 * slice_d
    count = small_params.shape[0]

    gathered = [
        lax.all_gather(jnp.stack([block_input[m], out_cotangent[m]]), "shard", axis=0)
        for m in range(micro_count)]

    small_lines = -(-count // (LANES * 16)) * 16
    small = jnp.pad(small_params, (0, small_lines * LANES - count)).reshape(small_lines, LANES)
    messages = cut_call(where, qkv_weight, up_weight, small, reps, shards)
    messages = [messages[0]] + [swap(messages[k], "shard", k) for k in range(1, shards)]
    lines = messages[0].shape[0] - small_lines
    piece = jnp.stack([message[:lines] for message in messages])
    mine, other = spread_pieces(piece, half)
    tables = []
    for m in range(micro_count):
        tables += [*rotation_tables(positions[m]),
                   visible_bias(segment_ids[m], positions[m], parent_ids[m, 0])]
    down_bf = down_weight.astype(BF16)
    attn_bf = attn_weight.astype(BF16)
    other, down_bf, attn_bf, *tables = tie(other, down_bf, attn_bf, *tables)
    weights = join_call(where, other, [join_call(where, mine, [], part)], part)
    weights = weights.reshape(width, -1)
    small_all = jnp.stack([message[lines:].reshape(-1)[:count] for message in messages])
    small_full = small_all[z ^ jnp.arange(shards)].reshape(-1).astype(F32)

    gain_one, bias_one, gain_two, bias_two = (
        small_full[i * width:(i + 1) * width].reshape(1, width) for i in range(4))
    qkv_bias = small_full[4 * width:7 * width].reshape(3, shards, pairs, PAIR)
    qkv_bias = lax.dynamic_index_in_dim(qkv_bias, z, 1, keepdims=False)
    qkv_bias = qkv_bias.transpose(1, 0, 2).reshape(1, qkv_cols)
    attn_bias = small_full[7 * width:8 * width]
    up_bias = lax.dynamic_slice_in_dim(
        small_full[8 * width:8 * width + hidden], z * slice_ff, slice_ff, 0).reshape(1, slice_ff)
    down_bias = small_full[8 * width + hidden:]
    out_bias = (attn_bias + down_bias).reshape(1, width)

    mlp_previous = None
    attn_previous = None
    sums_two = 0.0
    sums_one = 0.0
    summed = []
    for m in range(micro_count):
        xy = gathered[m]
        cosine, sine, mask = tables[3 * m:3 * m + 3]
        last = m == micro_count - 1
        if m > 0:
            sums_one, xy = tie(sums_one, xy)
        out_part, dx_part, *mlp_previous, sums = mlp_call(
            where, xy, gain_two, bias_two, up_bias, weights, down_bf, mlp_previous, reps, shards,
            qkv_cols)
        sums_two = sums_two + sums
        if last:
            mlp_keep, mlp_give, grad_up_bias = mlp_previous
            mlp_both = sum_cores(mlp_keep, mlp_give, half)
            mask, *mlp_both = tie(mask, *mlp_both)
        send, *attn_previous, sums = attn_call(
            where, xy, gain_one, bias_one, cosine, sine, mask, qkv_bias, weights, attn_bf,
            (out_part, dx_part), attn_previous, reps, shards)
        sums_one = sums_one + sums
        summed.append(lax.psum_scatter(send, "shard", scatter_dimension=0, tiled=False))

    all_tok = micro_count * rows * shards * reps
    rates = [rate / math.sqrt(all_tok) for rate in RATES]
    attn_keep, attn_give, grad_qkv_bias = attn_previous

    piece = sum_chips(mlp_both, half)
    piece, attn_give, sums_one = tie(piece, attn_give, sums_one)
    piece = exchange_columns(piece, width * slice_ff // reps // LANES, shards)
    attn_both = sum_cores(attn_keep, attn_give, half)
    mine, other = spread_pieces(piece, half)
    blocks = slice_ff // (256 if slice_ff % 256 == 0 and qkv_cols % 256 == 0 else 128)
    up_new, down_new, half_way, done = update_call(
        where, mine, other, (up_weight, up_moment, up_average),
        (down_weight, down_moment, down_average), [], blocks,
        (slice_ff, range(0, slice_ff, LANES)), (rates[2], rates[3]), shards)

    piece = sum_chips(attn_both, half)
    piece = exchange_columns(piece, width * qkv_cols // reps // LANES, shards)
    mine = spread_chips(piece, half)
    half_way, mine = tie(half_way, mine)
    other = swap(mine, "rep", 1)
    offsets = [which * width + pair * PAIR for pair in range(pairs) for which in range(3)]
    qkv_new, attn_new, *_ = update_call(
        where, mine, other, (qkv_weight, qkv_moment, qkv_average),
        (attn_weight, attn_moment, attn_average), [half_way, done], pairs, (slice_d, offsets),
        (rates[0], rates[1]), shards)

    head_part = jnp.concatenate(
        [sums_one[0], sums_one[1], sums_two[0], sums_two[1]])
    bias_part = lax.dynamic_update_slice(
        jnp.zeros((3, shards, slice_d), F32),
        grad_qkv_bias.reshape(pairs, 3, PAIR).transpose(1, 0, 2).reshape(3, 1, slice_d),
        (0, z, 0)).reshape(-1)
    token_part = jnp.where(z == 0, sums_two[2], 0.0)
    ff_part = lax.dynamic_update_slice(
        jnp.zeros((hidden,), F32), grad_up_bias.reshape(-1), (z * slice_ff,))
    small_grad = jnp.concatenate([head_part, bias_part, token_part, ff_part, token_part])
    small_grad = lax.all_gather(small_grad.reshape(-1, LANES), ("rep", "shard"), axis=0)
    small_grad = lax.dynamic_slice_in_dim(
        small_grad, z * (count // LANES), count // LANES, 1).sum(axis=0).reshape(-1)
    small_momentum = MOMENTUM * small_moment + small_grad
    small_weight = small_params - rates[4] * (small_grad + MOMENTUM * small_momentum)
    small_mean = AVERAGE_DECAY * small_average + (1.0 - AVERAGE_DECAY) * small_weight

    results = ()
    for m in range(micro_count):
        results = finish_call(m, block_input, out_cotangent, summed[m], out_bias, results)

    updated = (qkv_new, attn_new, up_new, down_new,
               (small_grad, jnp.stack([small_weight, small_mean]), small_momentum))
    return (*results, *(new[0] for new in updated), *(new[1] for new in updated),
            *(new[2] for new in updated))


def solution(mesh):
    tokens = P(None, ("rep", "shard"), None)
    tree = P(None, "rep")
    matrix = P("shard", None)
    vector = P("shard")
    weights = (matrix, matrix, matrix, matrix, vector)
    state = P(None, "shard", None)
    return jax.shard_map(
        local,
        mesh=mesh,
        in_specs=(tokens, tokens, tree, tree, P(None, "rep", None), *weights, *weights, *weights),
        out_specs=(tokens, tokens, *weights, state, state, state, state, P(None, "shard"),
                   *weights),
        check_vma=False,
    )
```

```python
from functools import partial
import math

import jax
import jax.numpy as jnp
import numpy as np
from jax import lax
from jax.experimental import pallas as pl
from jax.experimental.pallas import tpu as pltpu
from jax.sharding import PartitionSpec as P

HEAD = 64
ROT = 16
PAIR = 2 * HEAD
LANES = 128

EPSILON = 1e-05
NEGATIVE = -1e30
MOMENTUM = 0.5
AVERAGE_DECAY = 0.5
RATES = (0.045, 0.8, 0.1, 0.024, 0.4)

F32 = jnp.float32
BF16 = jnp.bfloat16
VMEM_LIMIT = 60 * 1024 * 1024
UPDATE_VMEM = 16 * 1024 * 1024
FINISH_VMEM = 8 * 1024 * 1024


def dot(a, b):
    return jnp.dot(a, b, preferred_element_type=F32)


def dot_t(a, b):
    return lax.dot_general(a, b, (((1,), (1,)), ((), ())), preferred_element_type=F32)


def normalize(values):
    center = values - jnp.mean(values, axis=-1, keepdims=True)
    spread = lax.rsqrt(jnp.mean(center * center, axis=-1, keepdims=True) + EPSILON)
    return center * spread, spread


def fixed(shape, index=None):
    zeros = (0,) * len(shape) if index is None else index
    return pl.BlockSpec(shape, lambda *_: zeros, pipeline_mode=pl.Buffered(1))


def small_lines(count):
    return -(-count // (LANES * 16)) * 16


def rows_of(ref):
    block = ref[...]
    return block.reshape(-1, block.shape[-1])


def mlp_kernel(first, reps, shards, where_ref, *refs):
    if first:
        (x_ref, dy_ref, gain_ref, bias_ref, ub_ref, up_ref, down_ref,
         out_ref, dx_ref, dup_ref, ddown_ref, dub_ref, sums_ref,
         hid, hid_t, unit, acc_out, acc_dx) = refs
    else:
        (x_ref, dy_ref, gain_ref, bias_ref, ub_ref, up_ref, down_ref, pup_ref, pdown_ref, pub_ref,
         out_ref, dx_ref, keep_ref, give_ref, dub_ref, sums_ref,
         hid, hid_t, unit, acc_out, acc_dx, dup_buf, ddown_buf) = refs
    step = pl.program_id(0)

    @pl.when(step == 0)
    def _():
        xhat, _ = normalize(rows_of(x_ref).astype(F32))
        unit[...] = xhat
        h = (xhat * gain_ref[...] + bias_ref[...]).astype(BF16)
        hid[...] = h
        hid_t[...] = h.T
        acc_out[...] = jnp.zeros_like(acc_out)
        acc_dx[...] = jnp.zeros_like(acc_dx)

    dy = rows_of(dy_ref)
    up = up_ref[...]
    down = down_ref[...]
    u = dot(hid[...], up) + ub_ref[...]
    cdf = 0.5 * (1.0 + lax.erf(u * (0.5 ** 0.5)))
    act = (u * cdf).astype(BF16)
    slope = cdf + u * (jnp.exp(-0.5 * u * u) * ((2.0 * math.pi) ** -0.5))
    dact = dot_t(dy, down)
    du32 = dact * slope
    du = du32.astype(BF16)
    acc_out[...] += dot(act, down)
    acc_dx[...] += dot_t(du, up)
    ddown = dot(act.T, dy)
    dup = dot(hid_t[...], du)
    dub = jnp.sum(du.astype(F32), axis=0, keepdims=True)
    if first:
        ddown_ref[...] = ddown
        dub_ref[...] = dub
        dup_ref[...] = dup
    else:
        dub_ref[...] = dub + pub_ref[...]
        dup_buf[...] = dup + pup_ref[...]
        ddown_buf[...] = ddown + pdown_ref[...]
        width, block = dup_buf.shape
        steps = pl.num_programs(0)
        part = width // shards // reps
        tiles = block // LANES
        line = block // reps
        up_rows = shards * steps * tiles * part
        for j in range(reps):
            piece = where_ref[0] ^ j
            out = keep_ref.at[j] if j < reps // 2 else give_ref.at[j - reps // 2]
            for zz in range(shards):
                row = (where_ref[1] ^ zz) * (width // shards) + piece * part
                value = dup_buf[pl.ds(pl.multiple_of(row, part), part), :].astype(BF16)
                for t in range(tiles):
                    at = ((zz * steps + step) * tiles + t) * part
                    out[pl.ds(pl.multiple_of(at, part), part), :] = (
                        value[:, t * LANES:(t + 1) * LANES])
            value = ddown_buf[pl.ds(pl.multiple_of(piece * line, line), line), :].astype(BF16)
            for t in range(width // LANES):
                at = up_rows + (step * (width // LANES) + t) * line
                out[pl.ds(pl.multiple_of(at, line), line), :] = value[:, t * LANES:(t + 1) * LANES]

    @pl.when(step == pl.num_programs(0) - 1)
    def _():
        dh = acc_dx[...]
        out_ref[...] = acc_out[...]
        dx_ref[...] = dh * gain_ref[...]
        sums_ref[0:1] = jnp.sum(dh * unit[...], axis=0, keepdims=True)
        sums_ref[1:2] = jnp.sum(dh, axis=0, keepdims=True)
        sums_ref[2:3] = jnp.sum(dy.astype(F32), axis=0, keepdims=True)
        sums_ref[3:8] = jnp.zeros((5, dh.shape[1]), F32)


def mlp_call(where, xy, gain, bias, up_bias, weights, down, previous, reps, shards, first_col):
    _, _, rows, width = xy.shape
    tokens = shards * rows
    hidden = down.shape[0]
    block = 256 if hidden % 256 == 0 and first_col % 256 == 0 else 128
    steps = hidden // block
    offset = first_col // block
    first = previous is None
    whole = lambda i, *_: (0, 0)
    in_specs = [
        fixed((shards, 1, rows, width)),
        fixed((shards, 1, rows, width), (0, 1, 0, 0)),
        fixed((1, width)),
        fixed((1, width)),
        pl.BlockSpec((1, block), lambda i, *_: (0, i)),
        pl.BlockSpec((width, block), lambda i, *_: (0, offset + i)),
        pl.BlockSpec((block, width), lambda i, *_: (i, 0)),
    ]
    args = [xy, xy, gain, bias, up_bias, weights, down]
    if first:
        grad_shapes = [jax.ShapeDtypeStruct((width, hidden), F32),
                       jax.ShapeDtypeStruct((hidden, width), F32)]
        grad_specs = [pl.BlockSpec((width, block), lambda i, *_: (0, i)),
                      pl.BlockSpec((block, width), lambda i, *_: (i, 0))]
        buffers = []
    else:
        in_specs += [
            pl.BlockSpec((width, block), lambda i, *_: (0, i)),
            pl.BlockSpec((block, width), lambda i, *_: (i, 0)),
            pl.BlockSpec((1, block), lambda i, *_: (0, i)),
        ]
        args += list(previous)
        pieces = (reps // 2, 2 * width * hidden // reps // LANES, LANES)
        grad_shapes = [jax.ShapeDtypeStruct(pieces, BF16)] * 2
        grad_specs = [pl.BlockSpec(pieces, lambda i, *_: (0, 0, 0))] * 2
        buffers = [pltpu.VMEM((width, block), F32), pltpu.VMEM((block, width), F32)]
    return pl.pallas_call(
        partial(mlp_kernel, first, reps, shards),
        grid_spec=pltpu.PrefetchScalarGridSpec(
            num_scalar_prefetch=1, grid=(steps,),
            in_specs=in_specs,
            out_specs=[
            pl.BlockSpec((tokens, width), whole),
            pl.BlockSpec((tokens, width), whole),
            *grad_specs,
            pl.BlockSpec((1, block), lambda i, *_: (0, i)),
            pl.BlockSpec((8, width), whole),
        ],
            scratch_shapes=[
                pltpu.VMEM((tokens, width), BF16),
                pltpu.VMEM((width, tokens), BF16),
                pltpu.VMEM((tokens, width), F32),
                pltpu.VMEM((tokens, width), F32),
                pltpu.VMEM((tokens, width), F32),
                *buffers,
            ]),
        out_shape=[
            jax.ShapeDtypeStruct((tokens, width), F32),
            jax.ShapeDtypeStruct((tokens, width), F32),
            *grad_shapes,
            jax.ShapeDtypeStruct((1, hidden), F32),
            jax.ShapeDtypeStruct((8, width), F32),
        ],
        compiler_params=pltpu.CompilerParams(
            dimension_semantics=("arbitrary",), vmem_limit_bytes=VMEM_LIMIT),
        cost_estimate=pl.CostEstimate(
            flops=12 * tokens * width * hidden, bytes_accessed=24 * 2**20,
            transcendentals=2 * tokens * hidden),
    )(where, *args)


def swap_halves(values):
    half = ROT // 2
    lane = lax.broadcasted_iota(jnp.int32, values.shape, 1) % HEAD
    return jnp.where(lane < half, pltpu.roll(values, PAIR - half, 1), pltpu.roll(values, half, 1))


def put_lines(ref, at, vector):
    for t in range(vector.shape[1] // LANES):
        ref[pl.ds(at + t, 1), :] = vector[:, t * LANES:(t + 1) * LANES]


def attn_kernel(first, reps, shards, where_ref, *refs):
    if first:
        (x_ref, dy_ref, gain_ref, bias_ref, cos_ref, sin_ref, mask_ref, qb_ref, qkv_ref, wo_ref,
         out_ref, dx_ref,
         send_ref, dqkv_ref, dwo_ref, dqb_ref, sums_ref,
         hid, hid_t, unit, acc_out, acc_dh) = refs
    else:
        (x_ref, dy_ref, gain_ref, bias_ref, cos_ref, sin_ref, mask_ref, qb_ref, qkv_ref, wo_ref,
         out_ref, dx_ref, pqkv_ref, pwo_ref, pqb_ref, psums_ref, msums_ref, dub_ref,
         send_ref, keep_ref, give_ref,
         hid, hid_t, unit, acc_out, acc_dh, dqkv_buf, dwo_buf, small) = refs
    step = pl.program_id(0)

    @pl.when(step == 0)
    def _():
        xhat, _ = normalize(rows_of(x_ref).astype(F32))
        unit[...] = xhat
        h = (xhat * gain_ref[...] + bias_ref[...]).astype(BF16)
        hid[...] = h
        hid_t[...] = h.T
        acc_out[...] = out_ref[...]
        acc_dh[...] = jnp.zeros_like(acc_dh)

    dy = rows_of(dy_ref)
    weights = qkv_ref[...]
    wo = wo_ref[...]
    cosine = cos_ref[...]
    sine = sin_ref[...]
    lin = dot(hid[...], weights) + qb_ref[...]
    q32 = lin[:, :PAIR]
    k32 = lin[:, PAIR:2 * PAIR]
    q = (q32 * cosine + swap_halves(q32) * sine).astype(BF16) * BF16(HEAD ** -0.5)
    k = (k32 * cosine + swap_halves(k32) * sine).astype(BF16)
    v = lin[:, 2 * PAIR:].astype(BF16)
    do = dot_t(dy, wo).astype(BF16)
    k_t = k.T
    v_t = v.T
    lane = lax.broadcasted_iota(jnp.int32, q.shape, 1)
    o_parts = []
    dq_parts = []
    dk = None
    dv = None
    tokens = q.shape[0]
    chunk = tokens if tokens <= 640 else tokens // 2
    for head in range(2):
        own = (lane // HEAD) == head
        q_h = jnp.where(own, q, jnp.zeros_like(q))
        do_h = jnp.where(own, do, jnp.zeros_like(do))
        part = slice(head * HEAD, (head + 1) * HEAD)
        o_row = []
        dq_row = []
        for at in range(0, tokens, chunk):
            q_c = q_h[at:at + chunk]
            do_c = do_h[at:at + chunk]
            scores = dot_t(k, q_c) + mask_ref[:, at:at + chunk]
            top = jnp.max(scores, axis=0, keepdims=True)
            e = jnp.exp(scores - top)
            prob = e * (1.0 / jnp.sum(e, axis=0, keepdims=True))
            prob_bf = prob.astype(BF16)
            o_row.append(dot(v_t[part], prob_bf))
            dprob = dot_t(v, do_c)
            weighted = prob * dprob
            delta = jnp.sum(weighted, axis=0, keepdims=True)
            ds = (weighted - prob * delta).astype(BF16)
            dq_row.append(dot(k_t[part], ds))
            dk_c = dot(ds, q_c)
            dv_c = dot(prob_bf, do_c)
            dk = dk_c if dk is None else dk + dk_c
            dv = dv_c if dv is None else dv + dv_c
        o_parts.append(jnp.concatenate(o_row, axis=1))
        dq_parts.append(jnp.concatenate(dq_row, axis=1))
    o_t = jnp.concatenate(o_parts, axis=0).astype(BF16)
    dq = jnp.concatenate(dq_parts, axis=0).T * (HEAD ** -0.5)
    dq = dq * cosine - swap_halves(dq) * sine
    dk = dk * cosine - swap_halves(dk) * sine
    dqkv = jnp.concatenate([dq.astype(BF16), dk.astype(BF16), dv.astype(BF16)], axis=1)
    acc_out[...] += dot(o_t.T, wo)
    acc_dh[...] += dot_t(dqkv, weights)
    dwo = dot(o_t, dy)
    dw = dot(hid_t[...], dqkv)
    dqb = jnp.sum(dqkv.astype(F32), axis=0, keepdims=True)
    if first:
        dwo_ref[...] = dwo
        dqkv_ref[...] = dw
        dqb_ref[...] = dqb
    else:
        dqb = dqb + pqb_ref[...]
        dqkv_buf[...] = dw + pqkv_ref[...]
        dwo_buf[...] = dwo + pwo_ref[...]
        width, cols = dqkv_buf.shape
        steps = pl.num_programs(0)

        @pl.when(step == 0)
        def _():
            small[...] = jnp.zeros_like(small)

        for which in range(3):
            put_lines(small, (4 + which) * (width // LANES) + where_ref[1] * steps + step,
                      dqb[:, which * PAIR:(which + 1) * PAIR])
        part = width // shards // reps
        line = PAIR // reps
        qkv_rows = shards * steps * 3 * part
        for j in range(reps):
            piece = where_ref[0] ^ j
            out = keep_ref.at[j] if j < reps // 2 else give_ref.at[j - reps // 2]
            for zz in range(shards):
                row = (where_ref[1] ^ zz) * (width // shards) + piece * part
                value = dqkv_buf[pl.ds(pl.multiple_of(row, part), part), :].astype(BF16)
                for t in range(3):
                    at = ((zz * steps + step) * 3 + t) * part
                    out[pl.ds(pl.multiple_of(at, part), part), :] = (
                        value[:, t * LANES:(t + 1) * LANES])
            value = dwo_buf[pl.ds(pl.multiple_of(piece * line, line), line), :].astype(BF16)
            for t in range(width // LANES):
                at = qkv_rows + (step * (width // LANES) + t) * line
                out[pl.ds(pl.multiple_of(at, line), line), :] = value[:, t * LANES:(t + 1) * LANES]

    @pl.when(step == pl.num_programs(0) - 1)
    def _():
        rows = send_ref.shape[2]
        width = send_ref.shape[3]
        dh = acc_dh[...]
        send_ref[:, 0] = acc_out[...].astype(BF16).reshape(shards, rows, width)
        send_ref[:, 1] = (dx_ref[...] + dh * gain_ref[...]).astype(BF16).reshape(
            shards, rows, width)
        sums = [jnp.sum(dh * unit[...], axis=0, keepdims=True), jnp.sum(dh, axis=0, keepdims=True)]
        if first:
            sums_ref[0:1] = sums[0]
            sums_ref[1:2] = sums[1]
            sums_ref[2:8] = jnp.zeros((6, width), F32)
        else:
            lines = width // LANES
            token = jnp.where(where_ref[1] == 0, msums_ref[2:3], 0.0)
            put_lines(small, 0, sums[0] + psums_ref[0:1])
            put_lines(small, lines, sums[1] + psums_ref[1:2])
            put_lines(small, 2 * lines, msums_ref[0:1])
            put_lines(small, 3 * lines, msums_ref[1:2])
            put_lines(small, 7 * lines, token)
            count = dub_ref.shape[1] // LANES
            put_lines(small, 8 * lines + where_ref[1] * count, dub_ref[...])
            put_lines(small, 8 * lines + shards * count, token)
            rounded = small[...].astype(BF16)
            end = keep_ref.shape[1] - rounded.shape[0]
            for j in range(reps // 2):
                keep_ref[j, end:, :] = rounded
                give_ref[j, end:, :] = rounded


def attn_call(where, xy, gain, bias, cosine, sine, mask, qkv_bias, weights, wo, partials, previous,
              reps, shards):
    _, _, rows, width = xy.shape
    tokens = shards * rows
    pairs = wo.shape[0] // PAIR
    cols = 3 * PAIR
    first = previous is None
    whole = lambda i, *_: (0, 0)
    in_specs = [
        fixed((shards, 1, rows, width)),
        fixed((shards, 1, rows, width), (0, 1, 0, 0)),
        fixed((1, width)),
        fixed((1, width)),
        fixed((tokens, PAIR)),
        fixed((tokens, PAIR)),
        fixed((tokens, tokens)),
        pl.BlockSpec((1, cols), lambda i, *_: (0, i)),
        pl.BlockSpec((width, cols), lambda i, *_: (0, i)),
        pl.BlockSpec((PAIR, width), lambda i, *_: (i, 0)),
        fixed((tokens, width)),
        fixed((tokens, width)),
    ]
    args = [xy, xy, gain, bias, cosine, sine, mask, qkv_bias, weights, wo, *partials]
    if first:
        grad_shapes = [jax.ShapeDtypeStruct((width, pairs * cols), F32),
                       jax.ShapeDtypeStruct((pairs * PAIR, width), F32)]
        grad_specs = [pl.BlockSpec((width, cols), lambda i, *_: (0, i)),
                      pl.BlockSpec((PAIR, width), lambda i, *_: (i, 0))]
        buffers = []
    else:
        in_specs += [
            pl.BlockSpec((width, cols), lambda i, *_: (0, i)),
            pl.BlockSpec((PAIR, width), lambda i, *_: (i, 0)),
            pl.BlockSpec((1, cols), lambda i, *_: (0, i)),
            *[fixed(array.shape) for array in previous[3:]],
        ]
        args += list(previous)
        small = small_lines(previous[5].shape[1] * shards + 9 * width)
        pieces = (reps // 2, width * pairs * (cols + PAIR) // reps // LANES + small, LANES)
        grad_shapes = [jax.ShapeDtypeStruct(pieces, BF16)] * 2
        grad_specs = [pl.BlockSpec(pieces, lambda i, *_: (0, 0, 0))] * 2
        buffers = [pltpu.VMEM((width, cols), F32), pltpu.VMEM((PAIR, width), F32),
                   pltpu.VMEM((small, LANES), F32)]
    return pl.pallas_call(
        partial(attn_kernel, first, reps, shards),
        grid_spec=pltpu.PrefetchScalarGridSpec(
            num_scalar_prefetch=1, grid=(pairs,),
            in_specs=in_specs,
            out_specs=[
            pl.BlockSpec((shards, 2, rows, width), lambda i, *_: (0, 0, 0, 0)),
            *grad_specs,
            *([pl.BlockSpec((1, cols), lambda i, *_: (0, i)),
               pl.BlockSpec((8, width), whole)] if first else []),
        ],
            scratch_shapes=[
                pltpu.VMEM((tokens, width), BF16),
                pltpu.VMEM((width, tokens), BF16),
                pltpu.VMEM((tokens, width), F32),
                pltpu.VMEM((tokens, width), F32),
                pltpu.VMEM((tokens, width), F32),
                *buffers,
            ]),
        out_shape=[
            jax.ShapeDtypeStruct((shards, 2, rows, width), BF16),
            *grad_shapes,
            *([jax.ShapeDtypeStruct((1, pairs * cols), F32),
               jax.ShapeDtypeStruct((8, width), F32)] if first else []),
        ],
        compiler_params=pltpu.CompilerParams(
            dimension_semantics=("arbitrary",), vmem_limit_bytes=VMEM_LIMIT),
        cost_estimate=pl.CostEstimate(
            flops=pairs * (6 * tokens * width * 4 * PAIR + 28 * tokens * tokens * PAIR),
            bytes_accessed=20 * 2**20, transcendentals=2 * pairs * tokens * tokens),
    )(where, *args)


def rotation_tables(pos_ids):
    half = ROT // 2
    lane = np.arange(PAIR) % HEAD
    frequency = 10000.0 ** (-(lane % half * 2.0) / ROT)
    per_lane = np.where(lane < ROT, frequency, 0.0).astype(np.float32)
    sign = np.where(lane < half, -1.0, np.where(lane < ROT, 1.0, 0.0)).astype(np.float32)
    angles = pos_ids.astype(F32)[:, None] * per_lane[None, :]
    return jnp.cos(angles), jnp.sin(angles) * sign[None, :]


def visible_bias(seg_ids, pos_ids, par_ids):
    labels = jnp.arange(par_ids.shape[0], dtype=jnp.int32)
    own = seg_ids[:, None] == labels[None, :]
    parent = jnp.sum(jnp.where(own, par_ids[None, :], 0), axis=1)
    parent_hot = parent[:, None] == labels[None, :]
    grand = jnp.sum(jnp.where(parent_hot, par_ids[None, :], 0), axis=1)
    key_seg = seg_ids[:, None]
    reach = (
        (key_seg == seg_ids[None, :])
        | (key_seg == parent[None, :])
        | (key_seg == grand[None, :])
    )
    return jnp.where(reach & (pos_ids[:, None] <= pos_ids[None, :]), 0.0, NEGATIVE).astype(F32)


def cut_kernel(shards, where_ref, qkv_ref, up_ref, small_ref, *out_refs):
    part, hidden = up_ref.shape
    width = qkv_ref.shape[1] // 3
    slice_d, slice_ff = width // shards, hidden // shards
    for zz in range(shards):
        out = out_refs[zz]
        there = where_ref[1] ^ zz
        at = 0
        for pair in range(slice_d // PAIR):
            for which in range(3):
                col = pl.multiple_of(there * slice_d, LANES) + (which * width + pair * PAIR)
                out[at:at + part, :] = qkv_ref[:, pl.ds(pl.multiple_of(col, LANES), LANES)].astype(BF16)
                at += part
        for tile in range(slice_ff // LANES):
            col = there * slice_ff + tile * LANES
            out[at:at + part, :] = up_ref[:, pl.ds(pl.multiple_of(col, LANES), LANES)].astype(BF16)
            at += part
        out[at:, :] = small_ref[...].astype(BF16)


def cut_call(where, qkv_weight, up_weight, small, reps, shards):
    owned, width3 = qkv_weight.shape
    hidden = up_weight.shape[1]
    part = owned // reps
    lines = (width3 + hidden) // shards // LANES * part + small.shape[0]
    shape = (lines, LANES)
    return pl.pallas_call(
        partial(cut_kernel, shards),
        grid_spec=pltpu.PrefetchScalarGridSpec(
            num_scalar_prefetch=1, grid=(1,),
            in_specs=[
                pl.BlockSpec((part, width3), lambda i, w: (w[0], 0)),
                pl.BlockSpec((part, hidden), lambda i, w: (w[0], 0)),
                pl.BlockSpec(small.shape, lambda i, w: (0, 0)),
            ],
            out_specs=[pl.BlockSpec(shape, lambda i, w: (0, 0))] * shards),
        out_shape=[jax.ShapeDtypeStruct(shape, BF16)] * shards,
    )(where, qkv_weight, up_weight, small)


def join_kernel(shards, where_ref, ref, out_ref):
    half, _, lines, _ = ref.shape
    _, _, part, cols = out_ref.shape
    for k in range(half):
        for zz in range(shards):
            for tile in range(cols // LANES):
                out_ref[where_ref[1] ^ zz, (where_ref[0] % half) ^ k, :,
                        tile * LANES:(tile + 1) * LANES] = (
                    ref[k, zz, tile * part:(tile + 1) * part, :])


def join_call(where, pieces, previous, part):
    half, shards, lines, _ = pieces.shape
    cols = lines // part * LANES
    other = len(previous)
    core = lambda w: (w[0] // half) ^ other

    def body(where_ref, ref, *refs):
        join_kernel(shards, where_ref, ref, refs[-1])

    return pl.pallas_call(
        body,
        grid_spec=pltpu.PrefetchScalarGridSpec(
            num_scalar_prefetch=1, grid=(1,),
            in_specs=[pl.BlockSpec(pieces.shape, lambda i, w: (0, 0, 0, 0))]
            + [pl.BlockSpec(memory_space=pl.ANY)] * other,
            out_specs=pl.BlockSpec((shards, half, part, cols), lambda i, w: (0, core(w), 0, 0))),
        out_shape=jax.ShapeDtypeStruct((shards, 2 * half, part, cols), BF16),
        input_output_aliases={2: 0} if other else {},
        compiler_params=pltpu.CompilerParams(vmem_limit_bytes=VMEM_LIMIT),
    )(where, pieces, *previous)


def update_kernel(shards, tiles, rates, where_ref, mine_ref, other_ref, *refs):
    *refs, token_ref, piece = refs
    refs = refs[:6] + refs[-6:]
    token_ref[...] = jnp.zeros_like(token_ref)
    step = pl.program_id(0)

    @pl.when(step < pl.num_programs(0) // 2)
    def _():
        piece[...] = mine_ref[0]

    @pl.when(step >= pl.num_programs(0) // 2)
    def _():
        piece[...] = other_ref[0]

    def one(weight, moment, average, grad, state, momentum, rate, lines, lead, lane):
        place = (*lead, slice(None), lane)
        g = lines.astype(F32)
        grad[place] = g
        m = MOMENTUM * moment[place] + g
        momentum[place] = m
        w = weight[place] - rate * (g + MOMENTUM * m)
        state[(0, *place)] = w
        state[(1, *place)] = AVERAGE_DECAY * average[place] + (1.0 - AVERAGE_DECAY) * w

    first, second = refs[:3] + refs[6:9], refs[3:6] + refs[9:]
    stride, offsets = tiles
    part = first[0].shape[0]
    at = 0
    for zz in range(shards):
        base = (where_ref[1] ^ zz) * stride
        for offset in offsets:
            lane = pl.ds(pl.multiple_of(base + offset, LANES), LANES)
            one(*first, rates[0], piece[at:at + part, :], (), lane)
            at += part
    count, _, line, width = second[0].shape
    for block in range(count):
        for t in range(width // LANES):
            one(*second, rates[1], piece[at:at + line, :], (block, 0),
                slice(t * LANES, (t + 1) * LANES))
            at += line


def fetch_kernel(count, *refs):
    ins, outs, token_ref, sems = refs[:count], refs[-count - 2:-2], refs[-2], refs[-1]
    copies = [pltpu.make_async_copy(ins[i], outs[i], sems.at[i]) for i in range(count)]
    for copy in copies:
        copy.start()
    token_ref[...] = jnp.zeros_like(token_ref)
    for copy in copies:
        copy.wait()


def fetch_call(arrays, after):
    count = len(arrays)
    anywhere = pl.BlockSpec(memory_space=pl.ANY)
    inside = pl.BlockSpec(memory_space=pltpu.VMEM)
    outs = pl.pallas_call(
        partial(fetch_kernel, count),
        in_specs=[anywhere] * (count + 1),
        out_specs=[inside] * (count + 1),
        out_shape=[pltpu.VMEM(array.shape, array.dtype) for array in arrays]
        + [jax.ShapeDtypeStruct((8, LANES), F32)],
        scratch_shapes=[pltpu.SemaphoreType.DMA((count,))],
        compiler_params=pltpu.CompilerParams(vmem_limit_bytes=FINISH_VMEM),
        cost_estimate=pl.CostEstimate(
            flops=0, bytes_accessed=sum(array.size for array in arrays) * 8, transcendentals=0),
    )(*[pltpu.with_memory_space_constraint(array, pltpu.HBM) for array in arrays], after)
    return outs[:count], outs[count]


def halves(reps, block):
    half = reps // 2
    rest = (0,) * (len(block) - 1)
    return [pl.BlockSpec(block, lambda i, w: (jnp.minimum(i, half - 1), *rest)),
            pl.BlockSpec(block, lambda i, w: (jnp.maximum(i - half, 0), *rest))]


def update_call(where, mine, other, first, second, after, blocks, tiles, rates, shards):
    half, lines, _ = mine.shape
    reps = 2 * half
    owned, cols = first[0].shape
    part = owned // reps
    depth, width = second[0].shape
    line = depth // blocks // reps
    second = [array.reshape(blocks, reps, line, width) for array in second]
    matrix = pl.BlockSpec((part, cols), lambda i, w: (w[0] ^ i, 0))
    quad = pl.BlockSpec((blocks, 1, line, width), lambda i, w: (0, w[0] ^ i, 0, 0))
    outs = pl.pallas_call(
        partial(update_kernel, shards, tiles, rates),
        grid_spec=pltpu.PrefetchScalarGridSpec(
            num_scalar_prefetch=1, grid=(reps,),
            in_specs=halves(reps, (1, lines, LANES)) + [matrix] * 3 + [quad] * 3
            + [pl.BlockSpec(memory_space=pl.ANY)] * len(after),
            out_specs=[
                matrix,
                pl.BlockSpec((2, part, cols), lambda i, w: (0, w[0] ^ i, 0)),
                matrix,
                quad,
                pl.BlockSpec((2, blocks, 1, line, width), lambda i, w: (0, 0, w[0] ^ i, 0, 0)),
                quad,
                pl.BlockSpec((8, LANES), lambda i, w: (0, 0)),
            ],
            scratch_shapes=[pltpu.VMEM((lines, LANES), BF16)]),
        out_shape=[
            jax.ShapeDtypeStruct((owned, cols), F32),
            jax.ShapeDtypeStruct((2, owned, cols), F32),
            jax.ShapeDtypeStruct((owned, cols), F32),
            jax.ShapeDtypeStruct((blocks, reps, line, width), F32),
            jax.ShapeDtypeStruct((2, blocks, reps, line, width), F32),
            jax.ShapeDtypeStruct((blocks, reps, line, width), F32),
            jax.ShapeDtypeStruct((8, LANES), F32),
        ],
        compiler_params=pltpu.CompilerParams(vmem_limit_bytes=UPDATE_VMEM),
        cost_estimate=pl.CostEstimate(
            flops=8 * (owned * cols + depth * width),
            bytes_accessed=30 * (owned * cols + depth * width), transcendentals=0),
    )(where, mine, other, *first, *second, *after)
    return (outs[:3],
            (outs[3].reshape(depth, width), outs[4].reshape(2, depth, width),
             outs[5].reshape(depth, width)), outs[6])


def finish_kernel(x_ref, dy_ref, sum_ref, bias_ref, *refs):
    out_ref, grad_ref = refs[-2:]
    x = x_ref[0].astype(F32)
    out_ref[0] = (x + sum_ref[0].astype(F32) + bias_ref[...]).astype(BF16)
    unit, spread = normalize(x)
    scaled = sum_ref[1].astype(F32)
    grad_ref[0] = dy_ref[0].astype(F32) + spread * (
        scaled - jnp.mean(scaled, axis=-1, keepdims=True)
        - unit * jnp.mean(scaled * unit, axis=-1, keepdims=True))


def finish_call(m, block_input, out_cotangent, summed, bias, previous, done):
    count, rows, width = block_input.shape
    one = pl.BlockSpec((1, rows, width), lambda i: (m, 0, 0))
    in_specs = [one, one, pl.BlockSpec((2, rows, width), lambda i: (0, 0, 0)),
                pl.BlockSpec((1, width), lambda i: (0, 0))]
    after = [*previous, done] if previous else []
    in_specs += [pl.BlockSpec(memory_space=pl.ANY)] * len(after)
    return pl.pallas_call(
        finish_kernel,
        grid=(1,),
        in_specs=in_specs,
        out_specs=[one, one],
        out_shape=[jax.ShapeDtypeStruct((count, rows, width), BF16),
                   jax.ShapeDtypeStruct((count, rows, width), F32)],
        input_output_aliases={4: 0, 5: 1} if previous else {},
        compiler_params=pltpu.CompilerParams(vmem_limit_bytes=FINISH_VMEM),
    )(block_input, out_cotangent, summed, bias, *after)


def swap(value, axis, mask):
    size = lax.axis_size(axis)
    return lax.ppermute(value, axis, [(i, i ^ mask) for i in range(size)])


def tie(*values):
    return lax.optimization_barrier(values)


def spread_chips(piece, half):
    return [swap(piece, "rep", 2 * k) for k in range(1, half)]


def spread_pieces(piece, half):
    mine = jnp.stack([piece, *spread_chips(piece, half)])
    return mine, swap(mine, "rep", 1)


def sum_cores(keep, give, half):
    other = swap(give, "rep", 1)
    both = [keep[k].astype(F32) + other[k].astype(F32) for k in range(half)]
    return both[:1] + [value.astype(BF16) for value in both[1:]]


def sum_chips(both, half):
    total = both[0]
    for k in range(1, half):
        total = total + swap(both[k], "rep", 2 * k).astype(F32)
    return total.astype(BF16)


def exchange_columns(piece, lines, small, shards):
    block = lines // shards
    end = piece.shape[0] - small
    messages = [piece[k * block:(k + 1) * block] for k in range(shards)]
    if small:
        messages = [jnp.concatenate([message, piece[end:]]) for message in messages]
    messages = messages[:1] + [swap(messages[k], "shard", k) for k in range(1, shards)]
    total = sum(message[block:].astype(F32) for message in messages)
    return jnp.concatenate([message[:block] for message in messages] + [piece[lines:end]]), total


def local(
    block_input,
    out_cotangent,
    segment_ids,
    positions,
    parent_ids,
    qkv_weight,
    attn_weight,
    up_weight,
    down_weight,
    small_params,
    qkv_moment,
    attn_moment,
    up_moment,
    down_moment,
    small_moment,
    qkv_average,
    attn_average,
    up_average,
    down_average,
    small_average,
):
    shards = lax.axis_size("shard")
    reps = lax.axis_size("rep")
    half = reps // 2
    rep = lax.axis_index("rep")
    z = lax.axis_index("shard")
    where = jnp.stack([(rep % 2) * half + rep // 2, z]).astype(jnp.int32)
    micro_count, rows, width = block_input.shape
    hidden = up_weight.shape[1]
    part = qkv_weight.shape[0] // reps
    slice_ff = hidden // shards
    slice_d = width // shards
    pairs = slice_d // PAIR
    qkv_cols = 3 * slice_d
    count = small_params.shape[0]

    gathered = [
        lax.all_gather(jnp.stack([block_input[m], out_cotangent[m]]), "shard", axis=0)
        for m in range(micro_count)]

    tail = small_lines(count)
    small = jnp.pad(small_params, (0, tail * LANES - count)).reshape(tail, LANES)
    messages = cut_call(where, qkv_weight, up_weight, small, reps, shards)
    messages = [messages[0]] + [swap(messages[k], "shard", k) for k in range(1, shards)]
    lines = messages[0].shape[0] - tail
    piece = jnp.stack([message[:lines] for message in messages])
    mine, other = spread_pieces(piece, half)
    tables = []
    for m in range(micro_count):
        tables += [*rotation_tables(positions[m]),
                   visible_bias(segment_ids[m], positions[m], parent_ids[m, 0])]
    down_bf = down_weight.astype(BF16)
    attn_bf = attn_weight.astype(BF16)
    other, down_bf, attn_bf, *tables = tie(other, down_bf, attn_bf, *tables)
    weights = join_call(where, other, [join_call(where, mine, [], part)], part)
    weights = weights.reshape(width, -1)
    small_all = jnp.stack([message[lines:].reshape(-1)[:count] for message in messages])
    small_full = small_all[z ^ jnp.arange(shards)].reshape(-1).astype(F32)

    gain_one, bias_one, gain_two, bias_two = (
        small_full[i * width:(i + 1) * width].reshape(1, width) for i in range(4))
    qkv_bias = small_full[4 * width:7 * width].reshape(3, shards, pairs, PAIR)
    qkv_bias = lax.dynamic_index_in_dim(qkv_bias, z, 1, keepdims=False)
    qkv_bias = qkv_bias.transpose(1, 0, 2).reshape(1, qkv_cols)
    attn_bias = small_full[7 * width:8 * width]
    up_bias = lax.dynamic_slice_in_dim(
        small_full[8 * width:8 * width + hidden], z * slice_ff, slice_ff, 0).reshape(1, slice_ff)
    down_bias = small_full[8 * width + hidden:]
    out_bias = (attn_bias + down_bias).reshape(1, width)

    mlp_previous = None
    attn_previous = None
    sums_two = 0.0
    summed = []
    for m in range(micro_count):
        xy = gathered[m]
        cosine, sine, mask = tables[3 * m:3 * m + 3]
        last = m == micro_count - 1
        if m > 0:
            *attn_previous, xy = tie(*attn_previous, xy)
        out_part, dx_part, *mlp_previous, sums = mlp_call(
            where, xy, gain_two, bias_two, up_bias, weights, down_bf, mlp_previous, reps, shards,
            qkv_cols)
        sums_two = sums_two + sums
        if last:
            mlp_keep, mlp_give, grad_up_bias = mlp_previous
            mlp_both = sum_cores(mlp_keep, mlp_give, half)
            small_at = (z * (count // LANES)).astype(jnp.uint32)
            mask, small_at, *mlp_both = tie(mask, small_at, *mlp_both)
            attn_previous = (*attn_previous, sums_two, grad_up_bias)
        send, *attn_previous = attn_call(
            where, xy, gain_one, bias_one, cosine, sine, mask, qkv_bias, weights, attn_bf,
            (out_part, dx_part), attn_previous, reps, shards)
        summed.append(lax.psum_scatter(send, "shard", scatter_dimension=0, tiled=False))

    all_tok = micro_count * rows * shards * reps
    rates = [rate / math.sqrt(all_tok) for rate in RATES]
    attn_keep, attn_give = attn_previous

    piece = sum_chips(mlp_both, half)
    piece, attn_give, summed[0] = tie(piece, attn_give, summed[0])
    attn_both = sum_cores(attn_keep, attn_give, half)
    piece, *attn_both = tie(piece, *attn_both)
    mlp_state, fetched = fetch_call(
        (up_weight, up_moment, up_average, down_weight, down_moment, down_average), attn_both[-1])
    mlp_piece, _ = exchange_columns(piece, width * slice_ff // reps // LANES, 0, shards)
    piece = sum_chips(attn_both, half)
    piece, mlp_piece, fetched = tie(piece, mlp_piece, fetched)
    piece, small_grad = exchange_columns(
        piece, width * qkv_cols // reps // LANES, small_lines(count * shards), shards)
    mlp_chips = spread_chips(mlp_piece, half)
    piece, *mlp_chips = tie(piece, *mlp_chips)
    chips = spread_chips(piece, half)

    mine = jnp.stack([mlp_piece, *mlp_chips])
    attn_state, fetched = fetch_call(
        (qkv_weight, qkv_moment, qkv_average, attn_weight, attn_moment, attn_average), fetched)
    other, fetched = tie(swap(mine, "rep", 1), fetched)
    blocks = slice_ff // (256 if slice_ff % 256 == 0 and qkv_cols % 256 == 0 else 128)
    up_new, down_new, done = update_call(
        where, mine, other, mlp_state[:3], mlp_state[3:], [fetched], blocks,
        (slice_ff, range(0, slice_ff, LANES)), (rates[2], rates[3]), shards)

    done, *chips = tie(done, *chips)
    mine = jnp.stack([piece, *chips])
    other = swap(mine, "rep", 1)
    offsets = [which * width + pair * PAIR for pair in range(pairs) for which in range(3)]
    qkv_new, attn_new, done = update_call(
        where, mine, other, attn_state[:3], attn_state[3:], [done], pairs, (slice_d, offsets),
        (rates[0], rates[1]), shards)
    done, summed[-1] = tie(done, summed[-1])

    small_grad = lax.dynamic_slice(
        small_grad, (small_at, jnp.uint32(0)), (count // LANES, LANES)).reshape(-1)
    small_momentum = MOMENTUM * small_moment + small_grad
    small_weight = small_params - rates[4] * (small_grad + MOMENTUM * small_momentum)
    small_mean = AVERAGE_DECAY * small_average + (1.0 - AVERAGE_DECAY) * small_weight

    results = ()
    for m in range(micro_count):
        results = finish_call(m, block_input, out_cotangent, summed[m], out_bias, results, done)

    updated = (qkv_new, attn_new, up_new, down_new,
               (small_grad, jnp.stack([small_weight, small_mean]), small_momentum))
    return (*results, *(new[0] for new in updated), *(new[1] for new in updated),
            *(new[2] for new in updated))


def solution(mesh):
    tokens = P(None, ("rep", "shard"), None)
    tree = P(None, "rep")
    matrix = P("shard", None)
    vector = P("shard")
    weights = (matrix, matrix, matrix, matrix, vector)
    state = P(None, "shard", None)
    return jax.shard_map(
        local,
        mesh=mesh,
        in_specs=(tokens, tokens, tree, tree, P(None, "rep", None), *weights, *weights, *weights),
        out_specs=(tokens, tokens, *weights, state, state, state, state, P(None, "shard"),
                   *weights),
        check_vma=False,
    )
```

```python
from functools import partial
import math

import jax
import jax.numpy as jnp
import numpy as np
from jax import lax
from jax.experimental import pallas as pl
from jax.experimental.pallas import tpu as pltpu
from jax.sharding import PartitionSpec as P

HEAD = 64
ROT = 16
PAIR = 2 * HEAD
LANES = 128

EPSILON = 1e-05
NEGATIVE = -1e30
MOMENTUM = 0.5
AVERAGE_DECAY = 0.5
RATES = (0.045, 0.8, 0.1, 0.024, 0.4)

F32 = jnp.float32
BF16 = jnp.bfloat16
VMEM_LIMIT = 60 * 1024 * 1024
UPDATE_VMEM = 16 * 1024 * 1024
FINISH_VMEM = 8 * 1024 * 1024


def dot(a, b):
    return jnp.dot(a, b, preferred_element_type=F32)


def dot_t(a, b):
    return lax.dot_general(a, b, (((1,), (1,)), ((), ())), preferred_element_type=F32)


def normalize(values):
    center = values - jnp.mean(values, axis=-1, keepdims=True)
    spread = lax.rsqrt(jnp.mean(center * center, axis=-1, keepdims=True) + EPSILON)
    return center * spread, spread


def fixed(shape, index=None):
    zeros = (0,) * len(shape) if index is None else index
    return pl.BlockSpec(shape, lambda *_: zeros, pipeline_mode=pl.Buffered(1))


def small_lines(count):
    return -(-count // (LANES * 16)) * 16


def rows_of(ref):
    block = ref[...]
    return block.reshape(-1, block.shape[-1])


def mlp_kernel(first, reps, shards, where_ref, *refs):
    if first:
        (x_ref, dy_ref, gain_ref, bias_ref, ub_ref, up_ref, down_ref,
         out_ref, dx_ref, dup_ref, ddown_ref, dub_ref, sums_ref,
         hid, hid_t, unit, acc_out, acc_dx) = refs
    else:
        (x_ref, dy_ref, gain_ref, bias_ref, ub_ref, up_ref, down_ref, pup_ref, pdown_ref, pub_ref,
         out_ref, dx_ref, keep_ref, give_ref, dub_ref, sums_ref,
         hid, hid_t, unit, acc_out, acc_dx, dup_buf, ddown_buf) = refs
    step = pl.program_id(0)

    @pl.when(step == 0)
    def _():
        xhat, _ = normalize(rows_of(x_ref).astype(F32))
        unit[...] = xhat
        h = (xhat * gain_ref[...] + bias_ref[...]).astype(BF16)
        hid[...] = h
        hid_t[...] = h.T
        acc_out[...] = jnp.zeros_like(acc_out)
        acc_dx[...] = jnp.zeros_like(acc_dx)

    dy = rows_of(dy_ref)
    up = up_ref[...]
    down = down_ref[...]
    u = dot(hid[...], up) + ub_ref[...]
    cdf = 0.5 * (1.0 + lax.erf(u * (0.5 ** 0.5)))
    act = (u * cdf).astype(BF16)
    slope = cdf + u * (jnp.exp(-0.5 * u * u) * ((2.0 * math.pi) ** -0.5))
    dact = dot_t(dy, down)
    du32 = dact * slope
    du = du32.astype(BF16)
    acc_out[...] += dot(act, down)
    acc_dx[...] += dot_t(du, up)
    ddown = dot(act.T, dy)
    dup = dot(hid_t[...], du)
    dub = jnp.sum(du.astype(F32), axis=0, keepdims=True)
    if first:
        ddown_ref[...] = ddown
        dub_ref[...] = dub
        dup_ref[...] = dup
    else:
        dub_ref[...] = dub + pub_ref[...]
        dup_buf[...] = dup + pup_ref[...]
        ddown_buf[...] = ddown + pdown_ref[...]
        width, block = dup_buf.shape
        steps = pl.num_programs(0)
        part = width // shards // reps
        tiles = block // LANES
        line = block // reps
        up_rows = shards * steps * tiles * part
        for j in range(reps):
            piece = where_ref[0] ^ j
            out = keep_ref.at[j] if j < reps // 2 else give_ref.at[j - reps // 2]
            for zz in range(shards):
                row = (where_ref[1] ^ zz) * (width // shards) + piece * part
                value = dup_buf[pl.ds(pl.multiple_of(row, part), part), :].astype(BF16)
                for t in range(tiles):
                    at = ((zz * steps + step) * tiles + t) * part
                    out[pl.ds(pl.multiple_of(at, part), part), :] = (
                        value[:, t * LANES:(t + 1) * LANES])
            value = ddown_buf[pl.ds(pl.multiple_of(piece * line, line), line), :].astype(BF16)
            for t in range(width // LANES):
                at = up_rows + (step * (width // LANES) + t) * line
                out[pl.ds(pl.multiple_of(at, line), line), :] = value[:, t * LANES:(t + 1) * LANES]

    @pl.when(step == pl.num_programs(0) - 1)
    def _():
        dh = acc_dx[...]
        out_ref[...] = acc_out[...]
        dx_ref[...] = dh * gain_ref[...]
        sums_ref[0:1] = jnp.sum(dh * unit[...], axis=0, keepdims=True)
        sums_ref[1:2] = jnp.sum(dh, axis=0, keepdims=True)
        sums_ref[2:3] = jnp.sum(dy.astype(F32), axis=0, keepdims=True)
        sums_ref[3:8] = jnp.zeros((5, dh.shape[1]), F32)


def mlp_call(where, xy, gain, bias, up_bias, weights, down, previous, reps, shards, first_col):
    _, _, rows, width = xy.shape
    tokens = shards * rows
    hidden = down.shape[0]
    block = 256 if hidden % 256 == 0 and first_col % 256 == 0 else 128
    steps = hidden // block
    offset = first_col // block
    first = previous is None
    whole = lambda i, *_: (0, 0)
    in_specs = [
        fixed((shards, 1, rows, width)),
        fixed((shards, 1, rows, width), (0, 1, 0, 0)),
        fixed((1, width)),
        fixed((1, width)),
        pl.BlockSpec((1, block), lambda i, *_: (0, i)),
        pl.BlockSpec((width, block), lambda i, *_: (0, offset + i)),
        pl.BlockSpec((block, width), lambda i, *_: (i, 0)),
    ]
    args = [xy, xy, gain, bias, up_bias, weights, down]
    if first:
        grad_shapes = [jax.ShapeDtypeStruct((width, hidden), F32),
                       jax.ShapeDtypeStruct((hidden, width), F32)]
        grad_specs = [pl.BlockSpec((width, block), lambda i, *_: (0, i)),
                      pl.BlockSpec((block, width), lambda i, *_: (i, 0))]
        buffers = []
    else:
        in_specs += [
            pl.BlockSpec((width, block), lambda i, *_: (0, i)),
            pl.BlockSpec((block, width), lambda i, *_: (i, 0)),
            pl.BlockSpec((1, block), lambda i, *_: (0, i)),
        ]
        args += list(previous)
        pieces = (reps // 2, 2 * width * hidden // reps // LANES, LANES)
        grad_shapes = [jax.ShapeDtypeStruct(pieces, BF16)] * 2
        grad_specs = [pl.BlockSpec(pieces, lambda i, *_: (0, 0, 0))] * 2
        buffers = [pltpu.VMEM((width, block), F32), pltpu.VMEM((block, width), F32)]
    return pl.pallas_call(
        partial(mlp_kernel, first, reps, shards),
        grid_spec=pltpu.PrefetchScalarGridSpec(
            num_scalar_prefetch=1, grid=(steps,),
            in_specs=in_specs,
            out_specs=[
            pl.BlockSpec((tokens, width), whole),
            pl.BlockSpec((tokens, width), whole),
            *grad_specs,
            pl.BlockSpec((1, block), lambda i, *_: (0, i)),
            pl.BlockSpec((8, width), whole),
        ],
            scratch_shapes=[
                pltpu.VMEM((tokens, width), BF16),
                pltpu.VMEM((width, tokens), BF16),
                pltpu.VMEM((tokens, width), F32),
                pltpu.VMEM((tokens, width), F32),
                pltpu.VMEM((tokens, width), F32),
                *buffers,
            ]),
        out_shape=[
            jax.ShapeDtypeStruct((tokens, width), F32),
            jax.ShapeDtypeStruct((tokens, width), F32),
            *grad_shapes,
            jax.ShapeDtypeStruct((1, hidden), F32),
            jax.ShapeDtypeStruct((8, width), F32),
        ],
        compiler_params=pltpu.CompilerParams(
            dimension_semantics=("arbitrary",), vmem_limit_bytes=VMEM_LIMIT),
        cost_estimate=pl.CostEstimate(
            flops=12 * tokens * width * hidden, bytes_accessed=24 * 2**20,
            transcendentals=2 * tokens * hidden),
    )(where, *args)


def swap_halves(values):
    half = ROT // 2
    lane = lax.broadcasted_iota(jnp.int32, values.shape, 1) % HEAD
    return jnp.where(lane < half, pltpu.roll(values, PAIR - half, 1), pltpu.roll(values, half, 1))


def put_lines(ref, at, vector):
    for t in range(vector.shape[1] // LANES):
        ref[pl.ds(at + t, 1), :] = vector[:, t * LANES:(t + 1) * LANES]


def attn_kernel(first, reps, shards, where_ref, *refs):
    if first:
        (x_ref, dy_ref, gain_ref, bias_ref, cos_ref, sin_ref, mask_ref, qb_ref, qkv_ref, wo_ref,
         out_ref, dx_ref,
         send_ref, dqkv_ref, dwo_ref, dqb_ref, sums_ref,
         hid, hid_t, unit, acc_out, acc_dh) = refs
    else:
        (x_ref, dy_ref, gain_ref, bias_ref, cos_ref, sin_ref, mask_ref, qb_ref, qkv_ref, wo_ref,
         out_ref, dx_ref, pqkv_ref, pwo_ref, pqb_ref, psums_ref, msums_ref, dub_ref,
         send_ref, keep_ref, give_ref,
         hid, hid_t, unit, acc_out, acc_dh, dqkv_buf, dwo_buf, small) = refs
    step = pl.program_id(0)

    @pl.when(step == 0)
    def _():
        xhat, _ = normalize(rows_of(x_ref).astype(F32))
        unit[...] = xhat
        h = (xhat * gain_ref[...] + bias_ref[...]).astype(BF16)
        hid[...] = h
        hid_t[...] = h.T
        acc_out[...] = out_ref[...]
        acc_dh[...] = jnp.zeros_like(acc_dh)

    dy = rows_of(dy_ref)
    weights = qkv_ref[...]
    wo = wo_ref[...]
    cosine = cos_ref[...]
    sine = sin_ref[...]
    lin = dot(hid[...], weights) + qb_ref[...]
    q32 = lin[:, :PAIR]
    k32 = lin[:, PAIR:2 * PAIR]
    q = (q32 * cosine + swap_halves(q32) * sine).astype(BF16) * BF16(HEAD ** -0.5)
    k = (k32 * cosine + swap_halves(k32) * sine).astype(BF16)
    v = lin[:, 2 * PAIR:].astype(BF16)
    do = dot_t(dy, wo).astype(BF16)
    k_t = k.T
    v_t = v.T
    lane = lax.broadcasted_iota(jnp.int32, q.shape, 1)
    o_parts = []
    dq_parts = []
    dk = None
    dv = None
    tokens = q.shape[0]
    chunk = tokens if tokens <= 640 else tokens // 2
    for head in range(2):
        own = (lane // HEAD) == head
        q_h = jnp.where(own, q, jnp.zeros_like(q))
        do_h = jnp.where(own, do, jnp.zeros_like(do))
        part = slice(head * HEAD, (head + 1) * HEAD)
        o_row = []
        dq_row = []
        for at in range(0, tokens, chunk):
            q_c = q_h[at:at + chunk]
            do_c = do_h[at:at + chunk]
            scores = dot_t(k, q_c) + mask_ref[:, at:at + chunk]
            top = jnp.max(scores, axis=0, keepdims=True)
            e = jnp.exp(scores - top)
            prob = e * (1.0 / jnp.sum(e, axis=0, keepdims=True))
            prob_bf = prob.astype(BF16)
            o_row.append(dot(v_t[part], prob_bf))
            dprob = dot_t(v, do_c)
            weighted = prob * dprob
            delta = jnp.sum(weighted, axis=0, keepdims=True)
            ds = (weighted - prob * delta).astype(BF16)
            dq_row.append(dot(k_t[part], ds))
            dk_c = dot(ds, q_c)
            dv_c = dot(prob_bf, do_c)
            dk = dk_c if dk is None else dk + dk_c
            dv = dv_c if dv is None else dv + dv_c
        o_parts.append(jnp.concatenate(o_row, axis=1))
        dq_parts.append(jnp.concatenate(dq_row, axis=1))
    o_t = jnp.concatenate(o_parts, axis=0).astype(BF16)
    dq = jnp.concatenate(dq_parts, axis=0).T * (HEAD ** -0.5)
    dq = dq * cosine - swap_halves(dq) * sine
    dk = dk * cosine - swap_halves(dk) * sine
    dqkv = jnp.concatenate([dq.astype(BF16), dk.astype(BF16), dv.astype(BF16)], axis=1)
    acc_out[...] += dot(o_t.T, wo)
    acc_dh[...] += dot_t(dqkv, weights)
    dwo = dot(o_t, dy)
    dw = dot(hid_t[...], dqkv)
    dqb = jnp.sum(dqkv.astype(F32), axis=0, keepdims=True)
    if first:
        dwo_ref[...] = dwo
        dqkv_ref[...] = dw
        dqb_ref[...] = dqb
    else:
        dqb = dqb + pqb_ref[...]
        dqkv_buf[...] = dw + pqkv_ref[...]
        dwo_buf[...] = dwo + pwo_ref[...]
        width, cols = dqkv_buf.shape
        steps = pl.num_programs(0)

        @pl.when(step == 0)
        def _():
            small[...] = jnp.zeros_like(small)

        for which in range(3):
            put_lines(small, (4 + which) * (width // LANES) + where_ref[1] * steps + step,
                      dqb[:, which * PAIR:(which + 1) * PAIR])
        part = width // shards // reps
        line = PAIR // reps
        qkv_rows = shards * steps * 3 * part
        for j in range(reps):
            piece = where_ref[0] ^ j
            out = keep_ref.at[j] if j < reps // 2 else give_ref.at[j - reps // 2]
            for zz in range(shards):
                row = (where_ref[1] ^ zz) * (width // shards) + piece * part
                value = dqkv_buf[pl.ds(pl.multiple_of(row, part), part), :].astype(BF16)
                for t in range(3):
                    at = ((zz * steps + step) * 3 + t) * part
                    out[pl.ds(pl.multiple_of(at, part), part), :] = (
                        value[:, t * LANES:(t + 1) * LANES])
            value = dwo_buf[pl.ds(pl.multiple_of(piece * line, line), line), :].astype(BF16)
            for t in range(width // LANES):
                at = qkv_rows + (step * (width // LANES) + t) * line
                out[pl.ds(pl.multiple_of(at, line), line), :] = value[:, t * LANES:(t + 1) * LANES]

    @pl.when(step == pl.num_programs(0) - 1)
    def _():
        rows = send_ref.shape[2]
        width = send_ref.shape[3]
        dh = acc_dh[...]
        send_ref[:, 0] = acc_out[...].astype(BF16).reshape(shards, rows, width)
        send_ref[:, 1] = (dx_ref[...] + dh * gain_ref[...]).astype(BF16).reshape(
            shards, rows, width)
        sums = [jnp.sum(dh * unit[...], axis=0, keepdims=True), jnp.sum(dh, axis=0, keepdims=True)]
        if first:
            sums_ref[0:1] = sums[0]
            sums_ref[1:2] = sums[1]
            sums_ref[2:8] = jnp.zeros((6, width), F32)
        else:
            lines = width // LANES
            token = jnp.where(where_ref[1] == 0, msums_ref[2:3], 0.0)
            put_lines(small, 0, sums[0] + psums_ref[0:1])
            put_lines(small, lines, sums[1] + psums_ref[1:2])
            put_lines(small, 2 * lines, msums_ref[0:1])
            put_lines(small, 3 * lines, msums_ref[1:2])
            put_lines(small, 7 * lines, token)
            count = dub_ref.shape[1] // LANES
            put_lines(small, 8 * lines + where_ref[1] * count, dub_ref[...])
            put_lines(small, 8 * lines + shards * count, token)
            rounded = small[...].astype(BF16)
            end = keep_ref.shape[1] - rounded.shape[0]
            for j in range(reps // 2):
                keep_ref[j, end:, :] = rounded
                give_ref[j, end:, :] = rounded


def attn_call(where, xy, gain, bias, cosine, sine, mask, qkv_bias, weights, wo, partials, previous,
              reps, shards):
    _, _, rows, width = xy.shape
    tokens = shards * rows
    pairs = wo.shape[0] // PAIR
    cols = 3 * PAIR
    first = previous is None
    whole = lambda i, *_: (0, 0)
    in_specs = [
        fixed((shards, 1, rows, width)),
        fixed((shards, 1, rows, width), (0, 1, 0, 0)),
        fixed((1, width)),
        fixed((1, width)),
        fixed((tokens, PAIR)),
        fixed((tokens, PAIR)),
        fixed((tokens, tokens)),
        pl.BlockSpec((1, cols), lambda i, *_: (0, i)),
        pl.BlockSpec((width, cols), lambda i, *_: (0, i)),
        pl.BlockSpec((PAIR, width), lambda i, *_: (i, 0)),
        fixed((tokens, width)),
        fixed((tokens, width)),
    ]
    args = [xy, xy, gain, bias, cosine, sine, mask, qkv_bias, weights, wo, *partials]
    if first:
        grad_shapes = [jax.ShapeDtypeStruct((width, pairs * cols), F32),
                       jax.ShapeDtypeStruct((pairs * PAIR, width), F32)]
        grad_specs = [pl.BlockSpec((width, cols), lambda i, *_: (0, i)),
                      pl.BlockSpec((PAIR, width), lambda i, *_: (i, 0))]
        buffers = []
    else:
        in_specs += [
            pl.BlockSpec((width, cols), lambda i, *_: (0, i)),
            pl.BlockSpec((PAIR, width), lambda i, *_: (i, 0)),
            pl.BlockSpec((1, cols), lambda i, *_: (0, i)),
            *[fixed(array.shape) for array in previous[3:]],
        ]
        args += list(previous)
        small = small_lines(previous[5].shape[1] * shards + 9 * width)
        pieces = (reps // 2, width * pairs * (cols + PAIR) // reps // LANES + small, LANES)
        grad_shapes = [jax.ShapeDtypeStruct(pieces, BF16)] * 2
        grad_specs = [pl.BlockSpec(pieces, lambda i, *_: (0, 0, 0))] * 2
        buffers = [pltpu.VMEM((width, cols), F32), pltpu.VMEM((PAIR, width), F32),
                   pltpu.VMEM((small, LANES), F32)]
    return pl.pallas_call(
        partial(attn_kernel, first, reps, shards),
        grid_spec=pltpu.PrefetchScalarGridSpec(
            num_scalar_prefetch=1, grid=(pairs,),
            in_specs=in_specs,
            out_specs=[
            pl.BlockSpec((shards, 2, rows, width), lambda i, *_: (0, 0, 0, 0)),
            *grad_specs,
            *([pl.BlockSpec((1, cols), lambda i, *_: (0, i)),
               pl.BlockSpec((8, width), whole)] if first else []),
        ],
            scratch_shapes=[
                pltpu.VMEM((tokens, width), BF16),
                pltpu.VMEM((width, tokens), BF16),
                pltpu.VMEM((tokens, width), F32),
                pltpu.VMEM((tokens, width), F32),
                pltpu.VMEM((tokens, width), F32),
                *buffers,
            ]),
        out_shape=[
            jax.ShapeDtypeStruct((shards, 2, rows, width), BF16),
            *grad_shapes,
            *([jax.ShapeDtypeStruct((1, pairs * cols), F32),
               jax.ShapeDtypeStruct((8, width), F32)] if first else []),
        ],
        compiler_params=pltpu.CompilerParams(
            dimension_semantics=("arbitrary",), vmem_limit_bytes=VMEM_LIMIT),
        cost_estimate=pl.CostEstimate(
            flops=pairs * (6 * tokens * width * 4 * PAIR + 28 * tokens * tokens * PAIR),
            bytes_accessed=20 * 2**20, transcendentals=2 * pairs * tokens * tokens),
    )(where, *args)


def rotation_tables(pos_ids):
    half = ROT // 2
    lane = np.arange(PAIR) % HEAD
    frequency = 10000.0 ** (-(lane % half * 2.0) / ROT)
    per_lane = np.where(lane < ROT, frequency, 0.0).astype(np.float32)
    sign = np.where(lane < half, -1.0, np.where(lane < ROT, 1.0, 0.0)).astype(np.float32)
    angles = pos_ids.astype(F32)[:, None] * per_lane[None, :]
    return jnp.cos(angles), jnp.sin(angles) * sign[None, :]


def visible_bias(seg_ids, pos_ids, par_ids):
    labels = jnp.arange(par_ids.shape[0], dtype=jnp.int32)
    own = seg_ids[:, None] == labels[None, :]
    parent = jnp.sum(jnp.where(own, par_ids[None, :], 0), axis=1)
    parent_hot = parent[:, None] == labels[None, :]
    grand = jnp.sum(jnp.where(parent_hot, par_ids[None, :], 0), axis=1)
    key_seg = seg_ids[:, None]
    reach = (
        (key_seg == seg_ids[None, :])
        | (key_seg == parent[None, :])
        | (key_seg == grand[None, :])
    )
    return jnp.where(reach & (pos_ids[:, None] <= pos_ids[None, :]), 0.0, NEGATIVE).astype(F32)


def cut_kernel(shards, where_ref, qkv_ref, up_ref, small_ref, *out_refs):
    part, hidden = up_ref.shape
    width = qkv_ref.shape[1] // 3
    slice_d, slice_ff = width // shards, hidden // shards
    for zz in range(shards):
        out = out_refs[zz]
        there = where_ref[1] ^ zz
        at = 0
        for pair in range(slice_d // PAIR):
            for which in range(3):
                col = pl.multiple_of(there * slice_d, LANES) + (which * width + pair * PAIR)
                out[at:at + part, :] = qkv_ref[:, pl.ds(pl.multiple_of(col, LANES), LANES)].astype(BF16)
                at += part
        for tile in range(slice_ff // LANES):
            col = there * slice_ff + tile * LANES
            out[at:at + part, :] = up_ref[:, pl.ds(pl.multiple_of(col, LANES), LANES)].astype(BF16)
            at += part
        out[at:, :] = small_ref[...].astype(BF16)


def cut_call(where, qkv_weight, up_weight, small, reps, shards):
    owned, width3 = qkv_weight.shape
    hidden = up_weight.shape[1]
    part = owned // reps
    lines = (width3 + hidden) // shards // LANES * part + small.shape[0]
    shape = (lines, LANES)
    return pl.pallas_call(
        partial(cut_kernel, shards),
        grid_spec=pltpu.PrefetchScalarGridSpec(
            num_scalar_prefetch=1, grid=(1,),
            in_specs=[
                pl.BlockSpec((part, width3), lambda i, w: (w[0], 0)),
                pl.BlockSpec((part, hidden), lambda i, w: (w[0], 0)),
                pl.BlockSpec(small.shape, lambda i, w: (0, 0)),
            ],
            out_specs=[pl.BlockSpec(shape, lambda i, w: (0, 0))] * shards),
        out_shape=[jax.ShapeDtypeStruct(shape, BF16)] * shards,
    )(where, qkv_weight, up_weight, small)


def join_kernel(shards, where_ref, ref, out_ref):
    half, _, lines, _ = ref.shape
    _, _, part, cols = out_ref.shape
    for k in range(half):
        for zz in range(shards):
            for tile in range(cols // LANES):
                out_ref[where_ref[1] ^ zz, (where_ref[0] % half) ^ k, :,
                        tile * LANES:(tile + 1) * LANES] = (
                    ref[k, zz, tile * part:(tile + 1) * part, :])


def join_call(where, pieces, previous, part):
    half, shards, lines, _ = pieces.shape
    cols = lines // part * LANES
    other = len(previous)
    core = lambda w: (w[0] // half) ^ other

    def body(where_ref, ref, *refs):
        join_kernel(shards, where_ref, ref, refs[-1])

    return pl.pallas_call(
        body,
        grid_spec=pltpu.PrefetchScalarGridSpec(
            num_scalar_prefetch=1, grid=(1,),
            in_specs=[pl.BlockSpec(pieces.shape, lambda i, w: (0, 0, 0, 0))]
            + [pl.BlockSpec(memory_space=pl.ANY)] * other,
            out_specs=pl.BlockSpec((shards, half, part, cols), lambda i, w: (0, core(w), 0, 0))),
        out_shape=jax.ShapeDtypeStruct((shards, 2 * half, part, cols), BF16),
        input_output_aliases={2: 0} if other else {},
        compiler_params=pltpu.CompilerParams(vmem_limit_bytes=VMEM_LIMIT),
    )(where, pieces, *previous)


def update_kernel(shards, tiles, rates, where_ref, mine_ref, other_ref, *refs):
    *refs, token_ref, piece = refs
    refs = refs[:6] + refs[-6:]
    token_ref[...] = jnp.zeros_like(token_ref)
    step = pl.program_id(0)

    @pl.when(step < pl.num_programs(0) // 2)
    def _():
        piece[...] = mine_ref[0]

    @pl.when(step >= pl.num_programs(0) // 2)
    def _():
        piece[...] = other_ref[0]

    def one(weight, moment, average, grad, state, momentum, rate, lines, lead, lane):
        place = (*lead, slice(None), lane)
        g = lines.astype(F32)
        grad[place] = g
        m = MOMENTUM * moment[place] + g
        momentum[place] = m
        w = weight[place] - rate * (g + MOMENTUM * m)
        state[(0, *place)] = w
        state[(1, *place)] = AVERAGE_DECAY * average[place] + (1.0 - AVERAGE_DECAY) * w

    first, second = refs[:3] + refs[6:9], refs[3:6] + refs[9:]
    stride, offsets = tiles
    part = first[0].shape[0]
    at = 0
    for zz in range(shards):
        base = (where_ref[1] ^ zz) * stride
        for offset in offsets:
            lane = pl.ds(pl.multiple_of(base + offset, LANES), LANES)
            one(*first, rates[0], piece[at:at + part, :], (), lane)
            at += part
    count, _, line, width = second[0].shape
    for block in range(count):
        for t in range(width // LANES):
            one(*second, rates[1], piece[at:at + line, :], (block, 0),
                slice(t * LANES, (t + 1) * LANES))
            at += line


def fetch_kernel(count, *refs):
    ins, outs, token_ref, sems = refs[:count], refs[-count - 2:-2], refs[-2], refs[-1]
    copies = [pltpu.make_async_copy(ins[i], outs[i], sems.at[i]) for i in range(count)]
    for copy in copies:
        copy.start()
    token_ref[...] = jnp.zeros_like(token_ref)
    for copy in copies:
        copy.wait()


def fetch_call(arrays, after):
    count = len(arrays)
    anywhere = pl.BlockSpec(memory_space=pl.ANY)
    inside = pl.BlockSpec(memory_space=pltpu.VMEM)
    outs = pl.pallas_call(
        partial(fetch_kernel, count),
        in_specs=[anywhere] * (count + 1),
        out_specs=[inside] * (count + 1),
        out_shape=[pltpu.VMEM(array.shape, array.dtype) for array in arrays]
        + [jax.ShapeDtypeStruct((8, LANES), F32)],
        scratch_shapes=[pltpu.SemaphoreType.DMA((count,))],
        compiler_params=pltpu.CompilerParams(vmem_limit_bytes=FINISH_VMEM),
        cost_estimate=pl.CostEstimate(
            flops=0, bytes_accessed=sum(array.size for array in arrays) * 8, transcendentals=0),
    )(*[pltpu.with_memory_space_constraint(array, pltpu.HBM) for array in arrays], after)
    return outs[:count], outs[count]


def halves(reps, block):
    half = reps // 2
    rest = (0,) * (len(block) - 1)
    return [pl.BlockSpec(block, lambda i, w: (jnp.minimum(i, half - 1), *rest)),
            pl.BlockSpec(block, lambda i, w: (jnp.maximum(i - half, 0), *rest))]


def update_call(where, mine, other, first, second, after, blocks, tiles, rates, shards):
    half, lines, _ = mine.shape
    reps = 2 * half
    owned, cols = first[0].shape
    part = owned // reps
    depth, width = second[0].shape
    line = depth // blocks // reps
    second = [array.reshape(blocks, reps, line, width) for array in second]
    matrix = pl.BlockSpec((part, cols), lambda i, w: (w[0] ^ i, 0))
    quad = pl.BlockSpec((blocks, 1, line, width), lambda i, w: (0, w[0] ^ i, 0, 0))
    outs = pl.pallas_call(
        partial(update_kernel, shards, tiles, rates),
        grid_spec=pltpu.PrefetchScalarGridSpec(
            num_scalar_prefetch=1, grid=(reps,),
            in_specs=halves(reps, (1, lines, LANES)) + [matrix] * 3 + [quad] * 3
            + [pl.BlockSpec(memory_space=pl.ANY)] * len(after),
            out_specs=[
                matrix,
                pl.BlockSpec((2, part, cols), lambda i, w: (0, w[0] ^ i, 0)),
                matrix,
                quad,
                pl.BlockSpec((2, blocks, 1, line, width), lambda i, w: (0, 0, w[0] ^ i, 0, 0)),
                quad,
                pl.BlockSpec((8, LANES), lambda i, w: (0, 0)),
            ],
            scratch_shapes=[pltpu.VMEM((lines, LANES), BF16)]),
        out_shape=[
            jax.ShapeDtypeStruct((owned, cols), F32),
            jax.ShapeDtypeStruct((2, owned, cols), F32),
            jax.ShapeDtypeStruct((owned, cols), F32),
            jax.ShapeDtypeStruct((blocks, reps, line, width), F32),
            jax.ShapeDtypeStruct((2, blocks, reps, line, width), F32),
            jax.ShapeDtypeStruct((blocks, reps, line, width), F32),
            jax.ShapeDtypeStruct((8, LANES), F32),
        ],
        compiler_params=pltpu.CompilerParams(vmem_limit_bytes=UPDATE_VMEM),
        cost_estimate=pl.CostEstimate(
            flops=8 * (owned * cols + depth * width),
            bytes_accessed=30 * (owned * cols + depth * width), transcendentals=0),
    )(where, mine, other, *first, *second, *after)
    return (outs[:3],
            (outs[3].reshape(depth, width), outs[4].reshape(2, depth, width),
             outs[5].reshape(depth, width)), outs[6])


def finish_kernel(x_ref, dy_ref, sum_ref, bias_ref, *refs):
    out_ref, grad_ref = refs[-2:]
    x = x_ref[0].astype(F32)
    out_ref[0] = (x + sum_ref[0].astype(F32) + bias_ref[...]).astype(BF16)
    unit, spread = normalize(x)
    scaled = sum_ref[1].astype(F32)
    grad_ref[0] = dy_ref[0].astype(F32) + spread * (
        scaled - jnp.mean(scaled, axis=-1, keepdims=True)
        - unit * jnp.mean(scaled * unit, axis=-1, keepdims=True))


def finish_call(m, block_input, out_cotangent, summed, bias, previous, done):
    count, rows, width = block_input.shape
    one = pl.BlockSpec((1, rows, width), lambda i: (m, 0, 0))
    in_specs = [one, one, pl.BlockSpec((2, rows, width), lambda i: (0, 0, 0)),
                pl.BlockSpec((1, width), lambda i: (0, 0))]
    after = [*previous, done] if previous else []
    in_specs += [pl.BlockSpec(memory_space=pl.ANY)] * len(after)
    return pl.pallas_call(
        finish_kernel,
        grid=(1,),
        in_specs=in_specs,
        out_specs=[one, one],
        out_shape=[jax.ShapeDtypeStruct((count, rows, width), BF16),
                   jax.ShapeDtypeStruct((count, rows, width), F32)],
        input_output_aliases={4: 0, 5: 1} if previous else {},
        compiler_params=pltpu.CompilerParams(vmem_limit_bytes=FINISH_VMEM),
    )(block_input, out_cotangent, summed, bias, *after)


def swap(value, axis, mask):
    size = lax.axis_size(axis)
    return lax.ppermute(value, axis, [(i, i ^ mask) for i in range(size)])


def tie(*values):
    return lax.optimization_barrier(values)


def spread_chips(piece, half):
    return [swap(piece, "rep", 2 * k) for k in range(1, half)]


def spread_pieces(piece, half):
    mine = jnp.stack([piece, *spread_chips(piece, half)])
    return mine, swap(mine, "rep", 1)


def sum_cores(keep, give, half):
    other = swap(give, "rep", 1)
    both = [keep[k].astype(F32) + other[k].astype(F32) for k in range(half)]
    return both[:1] + [value.astype(BF16) for value in both[1:]]


def sum_chips(both, half):
    total = both[0]
    for k in range(1, half):
        total = total + swap(both[k], "rep", 2 * k).astype(F32)
    return total.astype(BF16)


def exchange_columns(piece, lines, small, shards):
    block = lines // shards
    end = piece.shape[0] - small
    messages = [piece[k * block:(k + 1) * block] for k in range(shards)]
    if small:
        messages = [jnp.concatenate([message, piece[end:]]) for message in messages]
    messages = messages[:1] + [swap(messages[k], "shard", k) for k in range(1, shards)]
    total = sum(message[block:].astype(F32) for message in messages)
    return jnp.concatenate([message[:block] for message in messages] + [piece[lines:end]]), total


def local(
    block_input,
    out_cotangent,
    segment_ids,
    positions,
    parent_ids,
    qkv_weight,
    attn_weight,
    up_weight,
    down_weight,
    small_params,
    qkv_moment,
    attn_moment,
    up_moment,
    down_moment,
    small_moment,
    qkv_average,
    attn_average,
    up_average,
    down_average,
    small_average,
):
    shards = lax.axis_size("shard")
    reps = lax.axis_size("rep")
    half = reps // 2
    rep = lax.axis_index("rep")
    z = lax.axis_index("shard")
    where = jnp.stack([(rep % 2) * half + rep // 2, z]).astype(jnp.int32)
    micro_count, rows, width = block_input.shape
    hidden = up_weight.shape[1]
    part = qkv_weight.shape[0] // reps
    slice_ff = hidden // shards
    slice_d = width // shards
    pairs = slice_d // PAIR
    qkv_cols = 3 * slice_d
    count = small_params.shape[0]

    gathered = [
        lax.all_gather(jnp.stack([block_input[m], out_cotangent[m]]), "shard", axis=0)
        for m in range(micro_count)]

    tail = small_lines(count)
    small = jnp.pad(small_params, (0, tail * LANES - count)).reshape(tail, LANES)
    messages = cut_call(where, qkv_weight, up_weight, small, reps, shards)
    messages = [messages[0]] + [swap(messages[k], "shard", k) for k in range(1, shards)]
    lines = messages[0].shape[0] - tail
    piece = jnp.stack([message[:lines] for message in messages])
    mine, other = spread_pieces(piece, half)
    tables = []
    for m in range(micro_count):
        tables += [*rotation_tables(positions[m]),
                   visible_bias(segment_ids[m], positions[m], parent_ids[m, 0])]
    down_bf = down_weight.astype(BF16)
    attn_bf = attn_weight.astype(BF16)
    other, down_bf, attn_bf, *tables = tie(other, down_bf, attn_bf, *tables)
    weights = join_call(where, other, [join_call(where, mine, [], part)], part)
    weights = weights.reshape(width, -1)
    small_all = jnp.stack([message[lines:].reshape(-1)[:count] for message in messages])
    small_full = small_all[z ^ jnp.arange(shards)].reshape(-1).astype(F32)

    gain_one, bias_one, gain_two, bias_two = (
        small_full[i * width:(i + 1) * width].reshape(1, width) for i in range(4))
    qkv_bias = small_full[4 * width:7 * width].reshape(3, shards, pairs, PAIR)
    qkv_bias = lax.dynamic_index_in_dim(qkv_bias, z, 1, keepdims=False)
    qkv_bias = qkv_bias.transpose(1, 0, 2).reshape(1, qkv_cols)
    attn_bias = small_full[7 * width:8 * width]
    up_bias = lax.dynamic_slice_in_dim(
        small_full[8 * width:8 * width + hidden], z * slice_ff, slice_ff, 0).reshape(1, slice_ff)
    down_bias = small_full[8 * width + hidden:]
    out_bias = (attn_bias + down_bias).reshape(1, width)

    mlp_previous = None
    attn_previous = None
    sums_two = 0.0
    summed = []
    for m in range(micro_count):
        xy = gathered[m]
        cosine, sine, mask = tables[3 * m:3 * m + 3]
        last = m == micro_count - 1
        if m > 0:
            *attn_previous, xy = tie(*attn_previous, xy)
        out_part, dx_part, *mlp_previous, sums = mlp_call(
            where, xy, gain_two, bias_two, up_bias, weights, down_bf, mlp_previous, reps, shards,
            qkv_cols)
        sums_two = sums_two + sums
        if last:
            mlp_keep, mlp_give, grad_up_bias = mlp_previous
            mlp_both = sum_cores(mlp_keep, mlp_give, half)
            small_at = (z * (count // LANES)).astype(jnp.uint32)
            mask, small_at, *mlp_both = tie(mask, small_at, *mlp_both)
            attn_previous = (*attn_previous, sums_two, grad_up_bias)
        send, *attn_previous = attn_call(
            where, xy, gain_one, bias_one, cosine, sine, mask, qkv_bias, weights, attn_bf,
            (out_part, dx_part), attn_previous, reps, shards)
        summed.append(lax.psum_scatter(send, "shard", scatter_dimension=0, tiled=False))

    all_tok = micro_count * rows * shards * reps
    rates = [rate / math.sqrt(all_tok) for rate in RATES]
    attn_keep, attn_give = attn_previous

    piece = sum_chips(mlp_both, half)
    piece, attn_give, summed[0] = tie(piece, attn_give, summed[0])
    attn_both = sum_cores(attn_keep, attn_give, half)
    piece, *attn_both = tie(piece, *attn_both)
    mlp_state, fetched = fetch_call(
        (up_weight, up_moment, up_average, down_weight, down_moment, down_average), attn_both[-1])
    mlp_piece, _ = exchange_columns(piece, width * slice_ff // reps // LANES, 0, shards)
    piece = sum_chips(attn_both, half)
    piece, mlp_piece, fetched = tie(piece, mlp_piece, fetched)
    piece, small_grad = exchange_columns(
        piece, width * qkv_cols // reps // LANES, small_lines(count * shards), shards)
    mlp_chips = spread_chips(mlp_piece, half)
    piece, *mlp_chips = tie(piece, *mlp_chips)
    chips = spread_chips(piece, half)

    mine = jnp.stack([mlp_piece, *mlp_chips])
    attn_state, fetched = fetch_call(
        (qkv_weight, qkv_moment, attn_weight, attn_moment, attn_average), fetched)
    attn_state = [*attn_state[:2], qkv_average, *attn_state[2:]]
    other, fetched = tie(swap(mine, "rep", 1), fetched)
    blocks = slice_ff // (256 if slice_ff % 256 == 0 and qkv_cols % 256 == 0 else 128)
    up_new, down_new, done = update_call(
        where, mine, other, mlp_state[:3], mlp_state[3:], [fetched], blocks,
        (slice_ff, range(0, slice_ff, LANES)), (rates[2], rates[3]), shards)

    done, *chips = tie(done, *chips)
    mine = jnp.stack([piece, *chips])
    other = swap(mine, "rep", 1)
    offsets = [which * width + pair * PAIR for pair in range(pairs) for which in range(3)]
    qkv_new, attn_new, done = update_call(
        where, mine, other, attn_state[:3], attn_state[3:], [done], pairs, (slice_d, offsets),
        (rates[0], rates[1]), shards)
    done, summed[-1] = tie(done, summed[-1])

    small_grad = lax.dynamic_slice(
        small_grad, (small_at, jnp.uint32(0)), (count // LANES, LANES)).reshape(-1)
    small_momentum = MOMENTUM * small_moment + small_grad
    small_weight = small_params - rates[4] * (small_grad + MOMENTUM * small_momentum)
    small_mean = AVERAGE_DECAY * small_average + (1.0 - AVERAGE_DECAY) * small_weight

    results = ()
    for m in range(micro_count):
        results = finish_call(m, block_input, out_cotangent, summed[m], out_bias, results, done)

    updated = (qkv_new, attn_new, up_new, down_new,
               (small_grad, jnp.stack([small_weight, small_mean]), small_momentum))
    return (*results, *(new[0] for new in updated), *(new[1] for new in updated),
            *(new[2] for new in updated))


def solution(mesh):
    tokens = P(None, ("rep", "shard"), None)
    tree = P(None, "rep")
    matrix = P("shard", None)
    vector = P("shard")
    weights = (matrix, matrix, matrix, matrix, vector)
    state = P(None, "shard", None)
    return jax.shard_map(
        local,
        mesh=mesh,
        in_specs=(tokens, tokens, tree, tree, P(None, "rep", None), *weights, *weights, *weights),
        out_specs=(tokens, tokens, *weights, state, state, state, state, P(None, "shard"),
                   *weights),
        check_vma=False,
    )
```
